256 devices in a mesh: dom: 32 (over x, z), cls: 8 (over y, core).
Axes of the slice: x: 4, y: 4, z: 8, core: 2. Of those that a mesh axis runs over, the one named last changes fastest.
Arguments:
- images: bfloat16 [3072, 13824], P('dom')
- pick_counts: int32 [32], replicated, may hold values from 0 to 96, as said below
- group_of: int32 [3072], replicated, may hold values from 0 to 31
- ctf_table: float32 [32, 32], replicated, may hold values from -1 to 1
- precision: float32 [32], replicated, may hold values from 0.1 to 1
- references: bfloat16 [200, 13824], P('cls')
Outputs:
- new_refs: float32 [200, 13824], P('cls', 'dom')
- confidence: float32 [3072], P('dom')
The draws below stay inside these ranges and needn't reach their ends.
Inputs may be any that keep to these rules, and one draw needn't show every extreme that they name: `pick_counts`: the counts sum to 1536; each reader and the reader half of the dom axis away hold 96 particles together, and some reader holds exactly 96.
All inputs are finite; a program needn't handle non-finite values.
Results may differ from the reference program's by a relative error of at most 0.0037.
Values may be sent and summed in bfloat16 or wider, within the bound.
No kernel may reach another device: no remote copies, remote signals or barrier semaphores. Data moves between devices by JAX's collectives and lax.ppermute only.
A program may use at most 320 MiB of HBM per device.

```python
import math
import jax
import jax.numpy as jnp
from jax import lax

K = 200
ROT = 36
CYCLES = 32
ANG = 216
GROUPS = 32
OWN = 48
READ = 96
STEP = 6
FEAT = 13824
ROWS = 3072
N_DOM = 32


def make_classes(key):
    grid_shape = (K, CYCLES, ANG, 2)
    magnitude = math.sqrt(10.6 * math.log(ROT * K) / FEAT)
    class_gain = jax.random.uniform(jax.random.fold_in(key, 51), (K, 1, 1, 1), jnp.float32, 0.9, 1.1)
    entries = jax.random.uniform(jax.random.fold_in(key, 52), grid_shape, jnp.float32, 0.75, 1.25)
    cycle_gain = jax.random.uniform(jax.random.fold_in(key, 53), (K, CYCLES, 1, 1), jnp.float32, 0.85, 1.15)
    sign_field = (2 * jax.random.randint(jax.random.fold_in(key, 54), grid_shape, 0, 2) - 1).astype(jnp.float32)
    return magnitude * class_gain * cycle_gain * entries * sign_field


def make_ctf(key):
    return jax.random.uniform(jax.random.fold_in(key, 61), (GROUPS, CYCLES), jnp.float32, -1.0, 1.0)


def make_groups(key):
    return jax.random.randint(jax.random.fold_in(key, 62), (ROWS,), 0, GROUPS).astype(jnp.int32)


def rotate_rows(classes, chosen, turn_count):
    angle_index = (jnp.arange(ANG, dtype=jnp.int32)[None, :] - turn_count[:, None] * STEP) % ANG
    picked = classes[chosen[:, None], :, angle_index]
    return jnp.transpose(picked, (0, 2, 1, 3))


def make_images(key):
    classes = make_classes(key)
    ctf_values = make_ctf(key)
    groups = make_groups(key)
    grid_shape = (ROWS, CYCLES, ANG, 2)
    chosen = jax.random.randint(jax.random.fold_in(key, 71), (ROWS,), 0, K).astype(jnp.int32)
    turn_count = jax.random.randint(jax.random.fold_in(key, 72), (ROWS,), 0, ROT).astype(jnp.int32)
    ctf_rows = ctf_values[groups][:, :, None, None]
    signal = rotate_rows(classes, chosen, turn_count)
    noise_field = jnp.clip(jax.random.normal(jax.random.fold_in(key, 73), grid_shape, jnp.float32), -5.0, 5.0)
    drawn_rows = ctf_rows * signal + noise_field
    strong = jax.random.randint(jax.random.fold_in(key, 75), (ROWS,), 0, 32) == 0
    second_class = ((chosen + 1 + jax.random.randint(jax.random.fold_in(key, 76), (ROWS,), 0, K - 1)) % K).astype(jnp.int32)
    second_turn = jax.random.randint(jax.random.fold_in(key, 77), (ROWS,), 0, ROT).astype(jnp.int32)
    levels = jnp.array([16.0, 32.0, 48.0, 64.0], jnp.float32)
    strength = levels[jax.random.randint(jax.random.fold_in(key, 78), (ROWS,), 0, 4)]
    mixed_rows = strength[:, None, None, None] * ctf_rows * 0.5 * (signal + rotate_rows(classes, second_class, second_turn)) + 0.2 * noise_field
    return jnp.where(strong[:, None, None, None], mixed_rows, drawn_rows).reshape(ROWS, FEAT)


def draw_images(key, part):
    return make_images(key).astype(jnp.bfloat16)


def draw_references(key, part):
    return make_classes(key).reshape(K, FEAT).astype(jnp.bfloat16)


def draw_ctf_table(key, part):
    return make_ctf(key)


def draw_group_of(key, part):
    return make_groups(key)


def draw_pick_counts(key, part):
    half_axis = N_DOM // 2
    excess = jax.random.randint(jax.random.fold_in(key, 12), (half_axis,), 0, OWN + 1)
    full_pair = jax.random.randint(jax.random.fold_in(key, 13), (), 0, half_axis)
    excess = jnp.where(jnp.arange(half_axis, dtype=jnp.int32) == full_pair, OWN, excess)
    direction = 2 * jax.random.randint(jax.random.fold_in(key, 14), (half_axis,), 0, 2) - 1
    first_half = OWN + direction * excess
    second_half = OWN - direction * excess
    return jnp.concatenate([first_half, second_half]).astype(jnp.int32)


def setup_inputs(seed: int = 0) -> dict:
    key_of = jax.random.split(jax.random.key(seed), 7)
    images = draw_images(jax.random.fold_in(key_of[6], 71), 0)
    pick_counts = draw_pick_counts(jax.random.fold_in(key_of[6], 71), 0)
    group_of = draw_group_of(jax.random.fold_in(key_of[6], 71), 0)
    ctf_table = draw_ctf_table(jax.random.fold_in(key_of[6], 71), 0)
    precision = jnp.clip(jnp.exp(jax.random.uniform(key_of[4], (CYCLES,), jnp.float32, math.log(0.1), math.log(1.0))), 0.1, 1.0)
    references = draw_references(jax.random.fold_in(key_of[6], 71), 0)
    return {"images": images, "pick_counts": pick_counts, "group_of": group_of, "ctf_table": ctf_table, "precision": precision, "references": references}


ridge_term = 0.02


def reference(images, pick_counts, group_of, ctf_table, precision, references):
    total_rows = OWN * N_DOM
    ends_at = jnp.cumsum(pick_counts).astype(jnp.int32)
    starts = (ends_at - pick_counts).astype(jnp.int32)
    order_rank = jnp.arange(total_rows, dtype=jnp.int32)
    source = jnp.sum((ends_at[None, :] <= order_rank[:, None]).astype(jnp.int32), axis=1).astype(jnp.int32)
    position = order_rank - starts[source]
    flat_row = (source * READ + position).astype(jnp.int32)
    pixels = images[flat_row]
    groups = group_of[flat_row]
    ctf_rows = ctf_table[groups]
    cycle_scale = precision[None, :] * ctf_rows
    ctf_power = precision[None, :] * jnp.square(ctf_rows)
    shaped = pixels.reshape(total_rows, CYCLES, 2 * ANG).astype(jnp.float32)
    weighted = (cycle_scale[:, :, None] * shaped).astype(jnp.bfloat16).reshape(total_rows, FEAT)
    shaped_refs = references.reshape(K, CYCLES, 2 * ANG)
    energy = jnp.sum(jnp.square(shaped_refs.astype(jnp.float32)), axis=2)
    ref_power = jnp.dot(ctf_power, energy.T, precision=lax.Precision.HIGHEST)
    correlation = jnp.stack([jnp.dot(weighted, jnp.roll(shaped_refs, 2 * turn * STEP, axis=2).reshape(K, FEAT).T, preferred_element_type=jnp.float32) for turn in range(ROT)], axis=1)
    logits = correlation - 0.5 * ref_power[:, None, :]
    peak_logit = jnp.max(logits, axis=(1, 2))
    shifted = jnp.exp(logits - peak_logit[:, None, None])
    mass_total = jnp.sum(shifted, axis=(1, 2))
    posterior = shifted / mass_total[:, None, None]
    post_bf = posterior.astype(jnp.bfloat16)
    numerator = jnp.zeros((K, CYCLES, 2 * ANG), jnp.float32)
    for turn in range(ROT):
        partial_sum = jnp.dot(post_bf[:, turn, :].T, weighted, preferred_element_type=jnp.float32)
        numerator = numerator + jnp.roll(partial_sum.reshape(K, CYCLES, 2 * ANG), -2 * turn * STEP, axis=2)
    onehot = (groups[:, None] == jnp.arange(GROUPS, dtype=jnp.int32)[None, :]).astype(jnp.float32)
    weights = jnp.dot(jnp.sum(posterior, axis=1).T, onehot, precision=lax.Precision.HIGHEST)
    denominator = precision[None, :] * jnp.dot(weights, jnp.square(ctf_table), precision=lax.Precision.HIGHEST)
    new_refs = (numerator / (denominator[:, :, None] + ridge_term)).reshape(K, FEAT)
    confidence = jnp.zeros((READ * N_DOM,), jnp.float32).at[flat_row].set(1.0 / mass_total)
    return new_refs, confidence
```

```python
import functools

import jax
import jax.numpy as jnp
from jax import lax
from jax.experimental import pallas as pl
from jax.experimental.pallas import tpu as pltpu
from jax.sharding import PartitionSpec as P

ROT = 36
CYCLES = 32
ANG = 216
STEP = 6
FEAT = 13824
READ = 96
K_OWN = 25
GROUPS = 32

SPAN = 2 * ANG
HOP = 2 * STEP
N1 = 6
N2 = 6
CHUNKS = 4
CYC = 8
WIDE = CYC * SPAN
TILES = WIDE // 128
QP = 128
KP = 32
PACK = 104

ridge_term = 0.02
HIGH = lax.Precision.HIGHEST
X_SIZE, Z_SIZE = 4, 8

VM = pl.BlockSpec(memory_space=pltpu.VMEM)
SM = pl.BlockSpec(memory_space=pltpu.SMEM)
ANY = pl.BlockSpec(memory_space=pl.ANY)
PARAMS = pltpu.CompilerParams(vmem_limit_bytes=24 * 1024 * 1024)


def plan(sources):
    runs = []
    for lane, src in enumerate(sources):
        if src is None:
            continue
        key = (src // 128, (src - lane) % 128)
        if runs and runs[-1][2] == key and runs[-1][1] == lane:
            runs[-1][1] = lane + 1
        else:
            runs.append([lane, lane + 1, key])
    return sorted(runs, key=lambda run: run[0] - run[1])


def rolled_plan(shift):
    tiles = []
    for tile in range(TILES):
        sources = []
        for lane in range(128):
            cycle, place = divmod(128 * tile + lane, SPAN)
            sources.append(cycle * SPAN + (place + shift) % SPAN)
        tiles.append(plan(sources))
    return tiles


def packed_plan(cycle, part, shift):
    sources = []
    for lane in range(128):
        place = 128 * part + lane
        sources.append(cycle * SPAN + (place + shift) % SPAN if place < SPAN else None)
    return plan(sources)


def gather_tile(runs, load, lane, cache):
    value = None
    for first, last, (tile, turn) in runs:
        key = (tile, turn)
        if key not in cache:
            piece = load(tile)
            cache[key] = pltpu.roll(piece, 128 - turn, axis=1) if turn else piece
        piece = cache[key]
        if value is None:
            value = piece
            continue
        if first == 0:
            mask = lane < last
        elif last == 128:
            mask = lane >= first
        else:
            mask = (lane >= first) & (lane < last)
        value = jnp.where(mask, piece, value)
    return value


def match_kernel(
    images,
    refs,
    groups,
    table,
    precision,
    counts,
    stack,
    prob,
    stats,
    power_out,
    pix,
    raw,
    turned,
    scales,
    logits,
    sems,
):
    me = lax.axis_index("dom")
    copies = []
    for i in range(CHUNKS):
        span = pl.ds(i * WIDE, WIDE)
        copies.append(pltpu.make_async_copy(refs.at[:, span], raw.at[i], sems.at[0, i]))
        copies.append(pltpu.make_async_copy(images.at[:, span], pix.at[i], sems.at[1, i]))
    for copy in copies:
        copy.start()

    lane = lax.broadcasted_iota(jnp.int32, (8, QP), 1)
    base = me * READ
    row = base // 128
    off = base - row * 128
    turn = lax.rem(128 - off, 128)
    head = jnp.broadcast_to(groups[pl.ds(row, 1), :], (8, QP))
    tail = jnp.broadcast_to(groups[pl.ds(jnp.minimum(row + 1, 23), 1), :], (8, QP))
    mine = jnp.where(
        lane + off < 128, pltpu.roll(head, turn, axis=1), pltpu.roll(tail, turn, axis=1)
    )
    hot = (lax.broadcasted_iota(jnp.int32, (QP, QP), 0) == mine[0:1, :]).astype(jnp.float32)
    hot = hot.T[:, :GROUPS]
    ctf = jnp.dot(hot, table[...], precision=HIGH, preferred_element_type=jnp.float32)
    scale = precision[...] * ctf
    power = precision[...] * jnp.square(ctf)
    power_out[...] = power
    for i in range(CHUNKS):
        scales[i, :, 0:CYC] = scale[:, i * CYC : (i + 1) * CYC]

    logits[...] = jnp.zeros_like(logits)

    def chunk_step(i, energy):
        pltpu.make_async_copy(refs.at[:, pl.ds(0, WIDE)], raw.at[i], sems.at[0, i]).wait()
        lane_r = lax.broadcasted_iota(jnp.int32, (K_OWN, 128), 1)
        tiles = [raw[i, :, 128 * t : 128 * t + 128] for t in range(TILES)]
        for r2 in range(N2):
            cache = {}
            plans = rolled_plan((SPAN - N1 * HOP * r2) % SPAN)
            for t in range(TILES):
                turned[r2 * KP : r2 * KP + K_OWN, 128 * t : 128 * t + 128] = gather_tile(
                    plans[t], lambda u: tiles[u], lane_r, cache
                )
        lane_e = lax.broadcasted_iota(jnp.int32, (K_OWN, CYCLES), 1)
        sums = [None] * CYC
        for t in range(TILES):
            square = jnp.square(tiles[t].astype(jnp.float32))
            lo, hi = 128 * t // SPAN, (128 * t + 127) // SPAN
            parts = [(lo, square)]
            if hi != lo:
                edge = hi * SPAN - 128 * t
                parts = [
                    (lo, jnp.where(lane_r < edge, square, 0.0)),
                    (hi, jnp.where(lane_r >= edge, square, 0.0)),
                ]
            for c, part in parts:
                sums[c] = part if sums[c] is None else sums[c] + part
        for c in range(CYC):
            total = jnp.sum(sums[c], axis=1, keepdims=True)
            energy = jnp.where(lane_e == i * CYC + c, total, energy)

        pltpu.make_async_copy(images.at[:, pl.ds(0, WIDE)], pix.at[i], sems.at[1, i]).wait()
        for r1 in range(N1):
            stack[i, r1 * QP + READ : (r1 + 1) * QP, :] = jnp.zeros(
                (QP - READ, WIDE), jnp.bfloat16
            )

        def row_step(j, carry):
            rows = pl.ds(pl.multiple_of(j * 16, 16), 16)
            lane_w = lax.broadcasted_iota(jnp.int32, (16, 128), 1)
            factor = scales[i, rows, :]
            cols = [jnp.broadcast_to(factor[:, c : c + 1], (16, 128)) for c in range(CYC)]
            weighted = []
            for t in range(TILES):
                lo, hi = 128 * t // SPAN, (128 * t + 127) // SPAN
                amount = cols[lo]
                if hi != lo:
                    amount = jnp.where(lane_w < hi * SPAN - 128 * t, cols[lo], cols[hi])
                pixels = pix[i, rows, 128 * t : 128 * t + 128].astype(jnp.float32)
                weighted.append((amount * pixels).astype(jnp.bfloat16))
            for r1 in range(N1):
                cache = {}
                plans = rolled_plan(HOP * r1)
                out_rows = pl.ds(pl.multiple_of(r1 * QP + j * 16, 16), 16)
                for t in range(TILES):
                    stack[i, out_rows, 128 * t : 128 * t + 128] = gather_tile(
                        plans[t], lambda u: weighted[u], lane_w, cache
                    )
            return carry

        lax.fori_loop(0, READ // 16, row_step, 0)
        logits[...] += lax.dot_general(
            turned[...], stack[i], (((1,), (1,)), ((), ())), preferred_element_type=jnp.float32
        )
        return energy

    energy = lax.fori_loop(0, CHUNKS, chunk_step, jnp.zeros((K_OWN, CYCLES), jnp.float32))
    ref_power = lax.dot_general(
        energy,
        power,
        (((1,), (1,)), ((), ())),
        precision=HIGH,
        preferred_element_type=jnp.float32,
    )
    half = 0.5 * ref_power
    lane_q = lax.broadcasted_iota(jnp.int32, (K_OWN, QP), 1)
    alive = lane_q < counts[me]
    peak = jnp.full((K_OWN, QP), -3.0e38, jnp.float32)
    for r2 in range(N2):
        for r1 in range(N1):
            rows = slice(r2 * KP, r2 * KP + K_OWN)
            cols = slice(r1 * QP, (r1 + 1) * QP)
            value = jnp.where(alive, logits[rows, cols] - half, 0.0)
            logits[rows, cols] = value
            peak = jnp.maximum(peak, value)
    peak = jnp.max(peak, axis=0, keepdims=True)
    mass = jnp.zeros((K_OWN, QP), jnp.float32)
    prob[...] = jnp.zeros_like(prob)
    for r2 in range(N2):
        for r1 in range(N1):
            rows = slice(r2 * KP, r2 * KP + K_OWN)
            cols = slice(r1 * QP, (r1 + 1) * QP)
            value = jnp.exp(logits[rows, cols] - peak)
            prob[rows, cols] = value
            mass = mass + value
    mass = jnp.sum(mass, axis=0, keepdims=True)
    sub = lax.broadcasted_iota(jnp.int32, (8, QP), 0)
    block = jnp.where(sub == 0, peak, mass)
    for i in range(8):
        stats[i] = block


def scatter_chunk(stack, post, dens, partial, out, x_to):
    partial[...] = jnp.dot(post[...], stack[x_to], preferred_element_type=jnp.float32)
    lane = lax.broadcasted_iota(jnp.int32, (KP, 128), 1)
    caches = [{} for _ in range(N2)]
    for c in range(CYC):
        for part in range(4):
            total = None
            for r2 in range(N2):
                value = gather_tile(
                    packed_plan(c, part, N1 * HOP * r2),
                    lambda u: partial[r2 * KP : (r2 + 1) * KP, 128 * u : 128 * u + 128],
                    lane,
                    caches[r2],
                )
                total = value if total is None else total + value
            if part == 3:
                total = jnp.where(lane == SPAN - 384, dens[x_to][:, c : c + 1], total)
            out[c, K_OWN * part : K_OWN * (part + 1), :] = total[:K_OWN].astype(out.dtype)
        out[c, 4 * K_OWN : PACK, :] = jnp.zeros((PACK - 4 * K_OWN, 128), out.dtype)


def first_chunk_kernel(
    hop, stack, prob, stats, power, counts, out, post, dens, conf, partial
):
    me = lax.axis_index("dom")
    seat = lax.axis_index("cls")
    peak = stats[0][0:1, :]
    for i in range(1, 8):
        peak = jnp.maximum(peak, stats[i][0:1, :])
    mass = jnp.zeros((1, QP), jnp.float32)
    for i in range(8):
        mass = mass + stats[i][1:2, :] * jnp.exp(stats[i][0:1, :] - peak)
    alive = lax.broadcasted_iota(jnp.int32, (1, QP), 1) < counts[me]
    own_peak = stats[seat][0:1, :]
    factor = jnp.where(alive, jnp.exp(own_peak - peak) / mass, 0.0)
    conf[...] = jnp.broadcast_to(jnp.where(alive, 1.0 / mass, 0.0), conf.shape)
    total = jnp.zeros((KP, QP), jnp.float32)
    for r2 in range(N2):
        for r1 in range(N1):
            rows = slice(r2 * KP, (r2 + 1) * KP)
            cols = slice(r1 * QP, (r1 + 1) * QP)
            value = prob[rows, cols] * factor
            total = total + value
            post[rows, cols] = value.astype(jnp.bfloat16)
    den = jnp.dot(total, power[...], precision=HIGH, preferred_element_type=jnp.float32)
    for i in range(CHUNKS):
        dens[i, :, 0:CYC] = den[:, i * CYC : (i + 1) * CYC]
    scatter_chunk(stack, post, dens, partial, out, lax.rem(me // Z_SIZE + hop, X_SIZE))


def chunk_kernel(hop, stack, post, dens, out, partial):
    me = lax.axis_index("dom")
    scatter_chunk(stack, post, dens, partial, out, lax.rem(me // Z_SIZE + hop, X_SIZE))


def finish_kernel(pieces, out, acc):
    total = pieces[0].astype(jnp.float32)
    for i in range(1, Z_SIZE):
        total = total + pieces[i].astype(jnp.float32)
    acc[...] = total
    edge = SPAN - 384
    last = acc[3 * K_OWN : 4 * K_OWN, :]
    den = last[:, edge : edge + 1] + ridge_term
    for part in range(3):
        out[:, 128 * part : 128 * (part + 1)] = acc[K_OWN * part : K_OWN * (part + 1), :] / den
    out[:, 384:SPAN] = last[:, 0:edge] / den


def in_vmem(x):
    return pltpu.with_memory_space_constraint(x, pltpu.VMEM)


def body(images, pick_counts, group_of, ctf_table, precision, references):
    f32, bf16 = jnp.float32, jnp.bfloat16
    groups = group_of.reshape(24, 128)
    stack, prob, stats, power = pl.pallas_call(
        match_kernel,
        out_shape=(
            pltpu.VMEM((CHUNKS, N1 * QP, WIDE), bf16),
            pltpu.VMEM((N2 * KP, N1 * QP), f32),
            jax.ShapeDtypeStruct((8, 8, QP), f32),
            pltpu.VMEM((QP, CYCLES), f32),
        ),
        in_specs=[ANY, ANY, VM, VM, VM, SM],
        out_specs=(VM, VM, VM, VM),
        scratch_shapes=[
            pltpu.VMEM((CHUNKS, READ, WIDE), bf16),
            pltpu.VMEM((CHUNKS, K_OWN, WIDE), bf16),
            pltpu.VMEM((N2 * KP, WIDE), bf16),
            pltpu.VMEM((CHUNKS, QP, 128), f32),
            pltpu.VMEM((N2 * KP, N1 * QP), f32),
            pltpu.SemaphoreType.DMA((2, CHUNKS)),
        ],
        compiler_params=PARAMS,
        name="match",
    )(images, references, groups, ctf_table, precision.reshape(1, CYCLES), pick_counts)
    stats = lax.all_to_all(stats, "cls", 0, 0)
    stack, prob, power = in_vmem(stack), in_vmem(prob), in_vmem(power)

    part_shape = (CYC, PACK, 128)
    partial = pltpu.VMEM((N2 * KP, WIDE), f32)
    across, post, dens, conf = pl.pallas_call(
        functools.partial(first_chunk_kernel, 2),
        out_shape=(
            jax.ShapeDtypeStruct(part_shape, bf16),
            pltpu.VMEM((N2 * KP, N1 * QP), bf16),
            pltpu.VMEM((CHUNKS, KP, 128), f32),
            jax.ShapeDtypeStruct((8, QP), f32),
        ),
        in_specs=[VM, VM, VM, VM, SM],
        out_specs=(VM, VM, VM, VM),
        scratch_shapes=[partial],
        compiler_params=PARAMS,
        name="chunk2",
    )(stack, prob, stats, power, pick_counts)
    post, dens = in_vmem(post), in_vmem(dens)

    def moved(piece, hop):
        ring = [(j, (j // Z_SIZE + hop) % X_SIZE * Z_SIZE + j % Z_SIZE) for j in range(32)]
        return lax.ppermute(piece, "dom", ring)

    def chunk(hop, dtype):
        return pl.pallas_call(
            functools.partial(chunk_kernel, hop),
            out_shape=jax.ShapeDtypeStruct(part_shape, dtype),
            in_specs=[VM, VM, VM],
            out_specs=VM,
            scratch_shapes=[partial],
            compiler_params=PARAMS,
            name=f"chunk{hop}",
        )(stack, post, dens)

    got2 = moved(across, 2)
    got1 = moved(chunk(1, bf16), 1)
    got3 = moved(chunk(3, bf16), 3)
    own = chunk(0, f32)
    total = own + got1.astype(f32) + got2.astype(f32) + got3.astype(f32)
    z_groups = [[x * Z_SIZE + z for z in range(Z_SIZE)] for x in range(X_SIZE)]
    pieces = lax.all_to_all(total.astype(bf16), "dom", 0, 0, axis_index_groups=z_groups)
    new_refs = pl.pallas_call(
        finish_kernel,
        out_shape=jax.ShapeDtypeStruct((K_OWN, SPAN), f32),
        in_specs=[VM],
        out_specs=VM,
        scratch_shapes=[pltpu.VMEM((PACK, 128), f32)],
        compiler_params=PARAMS,
        name="finish",
    )(pieces)
    return new_refs, conf[0, :READ]


def solution(mesh):
    return jax.shard_map(
        body,
        mesh=mesh,
        in_specs=(P("dom", None), P(), P(), P(), P(), P("cls", None)),
        out_specs=(P("cls", "dom"), P("dom")),
        check_vma=False,
    )
```

```python
import functools

import jax
import jax.numpy as jnp
from jax import lax
from jax.experimental import pallas as pl
from jax.experimental.pallas import tpu as pltpu
from jax.sharding import PartitionSpec as P

ROT = 36
CYCLES = 32
ANG = 216
STEP = 6
FEAT = 13824
READ = 96
K_OWN = 25
GROUPS = 32

SPAN = 2 * ANG
HOP = 2 * STEP
N1 = 6
N2 = 6
CHUNKS = 4
CYC = 8
WIDE = CYC * SPAN
TILES = WIDE // 128
QP = 128
KP = 32
PACK = 104

ridge_term = 0.02
HIGH = lax.Precision.HIGHEST
X_SIZE, Z_SIZE = 4, 8

VM = pl.BlockSpec(memory_space=pltpu.VMEM)
FAR = pl.BlockSpec(memory_space=pltpu.HBM)
PARAMS = pltpu.CompilerParams(vmem_limit_bytes=12 * 1024 * 1024)


def plan(sources):
    runs = []
    for lane, src in enumerate(sources):
        if src is None:
            continue
        key = (src // 128, (src - lane) % 128)
        if runs and runs[-1][2] == key and runs[-1][1] == lane:
            runs[-1][1] = lane + 1
        else:
            runs.append([lane, lane + 1, key])
    return sorted(runs, key=lambda run: run[0] - run[1])


def rolled_plan(shift):
    tiles = []
    for tile in range(TILES):
        sources = []
        for lane in range(128):
            cycle, place = divmod(128 * tile + lane, SPAN)
            sources.append(cycle * SPAN + (place + shift) % SPAN)
        tiles.append(plan(sources))
    return tiles


def packed_plan(cycle, part, shift):
    sources = []
    for lane in range(128):
        place = 128 * part + lane
        sources.append(cycle * SPAN + (place + shift) % SPAN if place < SPAN else None)
    return plan(sources)


def gather_tile(runs, load, lane, cache):
    value = None
    for first, last, (tile, turn) in runs:
        key = (tile, turn)
        if key not in cache:
            piece = load(tile)
            cache[key] = pltpu.roll(piece, 128 - turn, axis=1) if turn else piece
        piece = cache[key]
        if value is None:
            value = piece
            continue
        if first == 0:
            mask = lane < last
        elif last == 128:
            mask = lane >= first
        else:
            mask = (lane >= first) & (lane < last)
        value = jnp.where(mask, piece, value)
    return value


def match_kernel(
    images,
    refs,
    groups_far,
    table_far,
    precision_far,
    counts_far,
    stack,
    prob,
    stats,
    power_out,
    pix,
    raw,
    turned,
    scales,
    logits,
    groups,
    table,
    precision,
    counts,
    sems,
    small_sems,
):
    me = lax.axis_index("dom")
    small = [
        pltpu.make_async_copy(src, dst, small_sems.at[n])
        for n, (src, dst) in enumerate(
            (
                (groups_far, groups),
                (table_far, table),
                (precision_far, precision),
                (counts_far, counts),
            )
        )
    ]
    for copy in small:
        copy.start()
    copies = []
    for i in range(CHUNKS):
        span = pl.ds(i * WIDE, WIDE)
        copies.append(pltpu.make_async_copy(refs.at[:, span], raw.at[i], sems.at[0, i]))
        copies.append(pltpu.make_async_copy(images.at[:, span], pix.at[i], sems.at[1, i]))
    for copy in copies:
        copy.start()
    for copy in small:
        copy.wait()

    lane = lax.broadcasted_iota(jnp.int32, (8, QP), 1)
    base = me * READ
    row = base // 128
    off = base - row * 128
    turn = lax.rem(128 - off, 128)
    head = jnp.broadcast_to(groups[pl.ds(row, 1), :], (8, QP))
    tail = jnp.broadcast_to(groups[pl.ds(jnp.minimum(row + 1, 23), 1), :], (8, QP))
    mine = jnp.where(
        lane + off < 128, pltpu.roll(head, turn, axis=1), pltpu.roll(tail, turn, axis=1)
    )
    hot = (lax.broadcasted_iota(jnp.int32, (QP, QP), 0) == mine[0:1, :]).astype(jnp.float32)
    hot = hot.T[:, :GROUPS]
    ctf = jnp.dot(hot, table[...], precision=HIGH, preferred_element_type=jnp.float32)
    scale = precision[...] * ctf
    power = precision[...] * jnp.square(ctf)
    power_out[...] = power
    for i in range(CHUNKS):
        scales[i, :, 0:CYC] = scale[:, i * CYC : (i + 1) * CYC]

    logits[...] = jnp.zeros_like(logits)

    def chunk_step(i, energy):
        pltpu.make_async_copy(refs.at[:, pl.ds(0, WIDE)], raw.at[i], sems.at[0, i]).wait()
        lane_r = lax.broadcasted_iota(jnp.int32, (K_OWN, 128), 1)
        tiles = [raw[i, :, 128 * t : 128 * t + 128] for t in range(TILES)]
        for r2 in range(N2):
            cache = {}
            plans = rolled_plan((SPAN - N1 * HOP * r2) % SPAN)
            for t in range(TILES):
                turned[r2 * KP : r2 * KP + K_OWN, 128 * t : 128 * t + 128] = gather_tile(
                    plans[t], lambda u: tiles[u], lane_r, cache
                )
        lane_e = lax.broadcasted_iota(jnp.int32, (K_OWN, CYCLES), 1)
        sums = [None] * CYC
        for t in range(TILES):
            square = jnp.square(tiles[t].astype(jnp.float32))
            lo, hi = 128 * t // SPAN, (128 * t + 127) // SPAN
            parts = [(lo, square)]
            if hi != lo:
                edge = hi * SPAN - 128 * t
                parts = [
                    (lo, jnp.where(lane_r < edge, square, 0.0)),
                    (hi, jnp.where(lane_r >= edge, square, 0.0)),
                ]
            for c, part in parts:
                sums[c] = part if sums[c] is None else sums[c] + part
        for c in range(CYC):
            total = jnp.sum(sums[c], axis=1, keepdims=True)
            energy = jnp.where(lane_e == i * CYC + c, total, energy)

        pltpu.make_async_copy(images.at[:, pl.ds(0, WIDE)], pix.at[i], sems.at[1, i]).wait()
        for r1 in range(N1):
            stack[i, r1 * QP + READ : (r1 + 1) * QP, :] = jnp.zeros(
                (QP - READ, WIDE), jnp.bfloat16
            )

        def row_step(j, carry):
            rows = pl.ds(pl.multiple_of(j * 16, 16), 16)
            lane_w = lax.broadcasted_iota(jnp.int32, (16, 128), 1)
            factor = scales[i, rows, :]
            cols = [jnp.broadcast_to(factor[:, c : c + 1], (16, 128)) for c in range(CYC)]
            weighted = []
            for t in range(TILES):
                lo, hi = 128 * t // SPAN, (128 * t + 127) // SPAN
                amount = cols[lo]
                if hi != lo:
                    amount = jnp.where(lane_w < hi * SPAN - 128 * t, cols[lo], cols[hi])
                pixels = pix[i, rows, 128 * t : 128 * t + 128].astype(jnp.float32)
                weighted.append((amount * pixels).astype(jnp.bfloat16))
            for r1 in range(N1):
                cache = {}
                plans = rolled_plan(HOP * r1)
                out_rows = pl.ds(pl.multiple_of(r1 * QP + j * 16, 16), 16)
                for t in range(TILES):
                    stack[i, out_rows, 128 * t : 128 * t + 128] = gather_tile(
                        plans[t], lambda u: weighted[u], lane_w, cache
                    )
            return carry

        lax.fori_loop(0, READ // 16, row_step, 0)
        logits[...] += lax.dot_general(
            turned[...], stack[i], (((1,), (1,)), ((), ())), preferred_element_type=jnp.float32
        )
        return energy

    energy = lax.fori_loop(0, CHUNKS, chunk_step, jnp.zeros((K_OWN, CYCLES), jnp.float32))
    ref_power = lax.dot_general(
        energy,
        power,
        (((1,), (1,)), ((), ())),
        precision=HIGH,
        preferred_element_type=jnp.float32,
    )
    half = 0.5 * ref_power
    lane_q = lax.broadcasted_iota(jnp.int32, (K_OWN, QP), 1)
    alive = lane_q < counts[me]
    peak = jnp.full((K_OWN, QP), -3.0e38, jnp.float32)
    for r2 in range(N2):
        for r1 in range(N1):
            rows = slice(r2 * KP, r2 * KP + K_OWN)
            cols = slice(r1 * QP, (r1 + 1) * QP)
            value = jnp.where(alive, logits[rows, cols] - half, 0.0)
            logits[rows, cols] = value
            peak = jnp.maximum(peak, value)
    peak = jnp.max(peak, axis=0, keepdims=True)
    mass = jnp.zeros((K_OWN, QP), jnp.float32)
    prob[...] = jnp.zeros_like(prob)
    for r2 in range(N2):
        for r1 in range(N1):
            rows = slice(r2 * KP, r2 * KP + K_OWN)
            cols = slice(r1 * QP, (r1 + 1) * QP)
            value = jnp.exp(logits[rows, cols] - peak)
            prob[rows, cols] = value
            mass = mass + value
    mass = jnp.sum(mass, axis=0, keepdims=True)
    sub = lax.broadcasted_iota(jnp.int32, (8, QP), 0)
    block = jnp.where(sub == 0, peak, jnp.where(alive[0:1, :], mass, 0.0))
    for i in range(8):
        stats[i] = block


def scatter_chunk(stack, post, dens, partial, out, x_to):
    partial[...] = jnp.dot(post[...], stack[x_to], preferred_element_type=jnp.float32)
    lane = lax.broadcasted_iota(jnp.int32, (KP, 128), 1)
    caches = [{} for _ in range(N2)]
    for c in range(CYC):
        for part in range(4):
            total = None
            for r2 in range(N2):
                value = gather_tile(
                    packed_plan(c, part, N1 * HOP * r2),
                    lambda u: partial[r2 * KP : (r2 + 1) * KP, 128 * u : 128 * u + 128],
                    lane,
                    caches[r2],
                )
                total = value if total is None else total + value
            if part == 3:
                total = jnp.where(lane == SPAN - 384, dens[x_to][:, c : c + 1], total)
            out[c, K_OWN * part : K_OWN * (part + 1), :] = total[:K_OWN].astype(out.dtype)
        out[c, 4 * K_OWN : PACK, :] = jnp.zeros((PACK - 4 * K_OWN, 128), out.dtype)


def first_chunk_kernel(
    hop, stack, prob, stats, power, out, post, dens, conf, partial
):
    me = lax.axis_index("dom")
    seat = lax.axis_index("cls")
    peak = stats[0][0:1, :]
    for i in range(1, 8):
        peak = jnp.maximum(peak, stats[i][0:1, :])
    mass = jnp.zeros((1, QP), jnp.float32)
    for i in range(8):
        mass = mass + stats[i][1:2, :] * jnp.exp(stats[i][0:1, :] - peak)
    alive = mass > 0.0
    own_peak = stats[seat][0:1, :]
    factor = jnp.where(alive, jnp.exp(own_peak - peak) / mass, 0.0)
    conf[...] = jnp.broadcast_to(jnp.where(alive, 1.0 / mass, 0.0), conf.shape)
    total = jnp.zeros((KP, QP), jnp.float32)
    for r2 in range(N2):
        for r1 in range(N1):
            rows = slice(r2 * KP, (r2 + 1) * KP)
            cols = slice(r1 * QP, (r1 + 1) * QP)
            value = prob[rows, cols] * factor
            total = total + value
            post[rows, cols] = value.astype(jnp.bfloat16)
    den = jnp.dot(total, power[...], precision=HIGH, preferred_element_type=jnp.float32)
    for i in range(CHUNKS):
        dens[i, :, 0:CYC] = den[:, i * CYC : (i + 1) * CYC]
    scatter_chunk(stack, post, dens, partial, out, lax.rem(me // Z_SIZE + hop, X_SIZE))


def chunk_kernel(hop, stack, post, dens, out, partial):
    me = lax.axis_index("dom")
    scatter_chunk(stack, post, dens, partial, out, lax.rem(me // Z_SIZE + hop, X_SIZE))


def finish_kernel(pieces, out, acc):
    total = pieces[0].astype(jnp.float32)
    for i in range(1, Z_SIZE):
        total = total + pieces[i].astype(jnp.float32)
    acc[...] = total
    edge = SPAN - 384
    last = acc[3 * K_OWN : 4 * K_OWN, :]
    den = last[:, edge : edge + 1] + ridge_term
    for part in range(3):
        out[:, 128 * part : 128 * (part + 1)] = acc[K_OWN * part : K_OWN * (part + 1), :] / den
    out[:, 384:SPAN] = last[:, 0:edge] / den


def in_hbm(x):
    return pltpu.with_memory_space_constraint(x, pltpu.HBM)


def in_vmem(x):
    return pltpu.with_memory_space_constraint(x, pltpu.VMEM)


def body(images, pick_counts, group_of, ctf_table, precision, references):
    f32, bf16 = jnp.float32, jnp.bfloat16
    operands = (
        images,
        references,
        group_of.reshape(24, 128),
        ctf_table,
        precision.reshape(1, CYCLES),
        pick_counts,
    )
    stack, prob, stats, power = pl.pallas_call(
        match_kernel,
        out_shape=(
            pltpu.VMEM((CHUNKS, N1 * QP, WIDE), bf16),
            pltpu.VMEM((N2 * KP, N1 * QP), f32),
            jax.ShapeDtypeStruct((8, 8, QP), f32),
            pltpu.VMEM((QP, CYCLES), f32),
        ),
        in_specs=[FAR] * 6,
        out_specs=(VM, VM, VM, VM),
        scratch_shapes=[
            pltpu.VMEM((CHUNKS, READ, WIDE), bf16),
            pltpu.VMEM((CHUNKS, K_OWN, WIDE), bf16),
            pltpu.VMEM((N2 * KP, WIDE), bf16),
            pltpu.VMEM((CHUNKS, QP, 128), f32),
            pltpu.VMEM((N2 * KP, N1 * QP), f32),
            pltpu.VMEM((24, 128), jnp.int32),
            pltpu.VMEM((GROUPS, CYCLES), f32),
            pltpu.VMEM((1, CYCLES), f32),
            pltpu.SMEM((32,), jnp.int32),
            pltpu.SemaphoreType.DMA((2, CHUNKS)),
            pltpu.SemaphoreType.DMA((4,)),
        ],
        compiler_params=PARAMS,
        name="match",
    )(*map(in_hbm, operands))
    stats = lax.all_to_all(stats, "cls", 0, 0)
    stack, prob, power = in_vmem(stack), in_vmem(prob), in_vmem(power)

    part_shape = (CYC, PACK, 128)
    partial = pltpu.VMEM((N2 * KP, WIDE), f32)
    across, post, dens, conf = pl.pallas_call(
        functools.partial(first_chunk_kernel, 2),
        out_shape=(
            jax.ShapeDtypeStruct(part_shape, bf16),
            pltpu.VMEM((N2 * KP, N1 * QP), bf16),
            pltpu.VMEM((CHUNKS, KP, 128), f32),
            jax.ShapeDtypeStruct((8, QP), f32),
        ),
        in_specs=[VM, VM, VM, VM],
        out_specs=(VM, VM, VM, VM),
        scratch_shapes=[partial],
        compiler_params=PARAMS,
        name="chunk2",
    )(stack, prob, stats, power)
    post, dens = in_vmem(post), in_vmem(dens)

    def moved(piece, hop):
        ring = [(j, (j // Z_SIZE + hop) % X_SIZE * Z_SIZE + j % Z_SIZE) for j in range(32)]
        return lax.ppermute(piece, "dom", ring)

    def chunk(hop, dtype):
        return pl.pallas_call(
            functools.partial(chunk_kernel, hop),
            out_shape=jax.ShapeDtypeStruct(part_shape, dtype),
            in_specs=[VM, VM, VM],
            out_specs=VM,
            scratch_shapes=[partial],
            compiler_params=PARAMS,
            name=f"chunk{hop}",
        )(stack, post, dens)

    got2 = moved(across, 2)
    got1 = moved(chunk(1, bf16), 1)
    got3 = moved(chunk(3, bf16), 3)
    own = chunk(0, f32)
    total = own + got1.astype(f32) + got2.astype(f32) + got3.astype(f32)
    z_groups = [[x * Z_SIZE + z for z in range(Z_SIZE)] for x in range(X_SIZE)]
    pieces = lax.all_to_all(total.astype(bf16), "dom", 0, 0, axis_index_groups=z_groups)
    new_refs = pl.pallas_call(
        finish_kernel,
        out_shape=jax.ShapeDtypeStruct((K_OWN, SPAN), f32),
        in_specs=[VM],
        out_specs=VM,
        scratch_shapes=[pltpu.VMEM((PACK, 128), f32)],
        compiler_params=PARAMS,
        name="finish",
    )(pieces)
    return new_refs, conf[0, :READ]


def solution(mesh):
    return jax.shard_map(
        body,
        mesh=mesh,
        in_specs=(P("dom", None), P(), P(), P(), P(), P("cls", None)),
        out_specs=(P("cls", "dom"), P("dom")),
        check_vma=False,
    )
```

```python
import functools

import jax
import jax.numpy as jnp
from jax import lax
from jax.experimental import pallas as pl
from jax.experimental.pallas import tpu as pltpu
from jax.sharding import PartitionSpec as P


CYCLES = 32
ANG = 216
STEP = 6
READ = 96
K_OWN = 25
GROUPS = 32

SPAN = 2 * ANG
HOP = 2 * STEP
N1 = 6
N2 = 6
CHUNKS = 4
CYC = 8
WIDE = CYC * SPAN
TILES = WIDE // 128
EDGE = SPAN - 384
QP = 128
KP = 32
LOW = 13
PACK = 3 * K_OWN + LOW

ridge_term = 0.02
HIGH = lax.Precision.HIGHEST
X_SIZE, Z_SIZE = 4, 8

VM = pl.BlockSpec(memory_space=pltpu.VMEM)
FAR = pl.BlockSpec(memory_space=pltpu.HBM)
PARAMS = pltpu.CompilerParams(vmem_limit_bytes=12 * 1024 * 1024)


def plan(sources):
    runs = []
    for lane, src in enumerate(sources):
        if src is None:
            continue
        key = (src // 128, (src - lane) % 128)
        if runs and runs[-1][2] == key and runs[-1][1] == lane:
            runs[-1][1] = lane + 1
        else:
            runs.append([lane, lane + 1, key])
    return sorted(runs, key=lambda run: run[0] - run[1])


def rolled_plan(shift):
    tiles = []
    for tile in range(TILES):
        sources = []
        for lane in range(128):
            cycle, place = divmod(128 * tile + lane, SPAN)
            sources.append(cycle * SPAN + (place + shift) % SPAN)
        tiles.append(plan(sources))
    return tiles


def packed_plan(cycle, part, shift):
    sources = []
    for lane in range(128):
        place = 128 * part + lane
        sources.append(cycle * SPAN + (place + shift) % SPAN if place < SPAN else None)
    return plan(sources)


def gather_tile(runs, load, lane, cache):
    value = None
    for first, last, (tile, turn) in runs:
        key = (tile, turn)
        if key not in cache:
            piece = load(tile)
            cache[key] = pltpu.roll(piece, 128 - turn, axis=1) if turn else piece
        piece = cache[key]
        if value is None:
            value = piece
            continue
        if first == 0:
            mask = lane < last
        elif last == 128:
            mask = lane >= first
        else:
            mask = (lane >= first) & (lane < last)
        value = jnp.where(mask, piece, value)
    return value


def match_kernel(
    images,
    refs,
    groups_far,
    table_far,
    precision_far,
    counts_far,
    stack,
    prob,
    stats,
    power_out,
    pix,
    raw,
    turned,
    scales,
    logits,
    groups,
    table,
    precision,
    counts,
    sems,
    small_sems,
):
    me = lax.axis_index("dom")
    small = [
        pltpu.make_async_copy(src, dst, small_sems.at[n])
        for n, (src, dst) in enumerate(
            (
                (groups_far, groups),
                (table_far, table),
                (precision_far, precision),
                (counts_far, counts),
            )
        )
    ]
    for copy in small:
        copy.start()
    copies = []
    for i in range(CHUNKS):
        span = pl.ds(i * WIDE, WIDE)
        copies.append(pltpu.make_async_copy(refs.at[:, span], raw.at[i], sems.at[0, i]))
        copies.append(pltpu.make_async_copy(images.at[:, span], pix.at[i], sems.at[1, i]))
    for copy in copies:
        copy.start()
    for copy in small:
        copy.wait()

    lane = lax.broadcasted_iota(jnp.int32, (8, QP), 1)
    base = me * READ
    row = base // 128
    off = base - row * 128
    turn = lax.rem(128 - off, 128)
    head = jnp.broadcast_to(groups[pl.ds(row, 1), :], (8, QP))
    tail = jnp.broadcast_to(groups[pl.ds(jnp.minimum(row + 1, 23), 1), :], (8, QP))
    mine = jnp.where(
        lane + off < 128, pltpu.roll(head, turn, axis=1), pltpu.roll(tail, turn, axis=1)
    )
    hot = (lax.broadcasted_iota(jnp.int32, (QP, QP), 0) == mine[0:1, :]).astype(jnp.float32)
    hot = hot.T[:, :GROUPS]
    ctf = jnp.dot(hot, table[...], precision=HIGH, preferred_element_type=jnp.float32)
    scale = precision[...] * ctf
    power = precision[...] * jnp.square(ctf)
    power_out[...] = power
    for i in range(CHUNKS):
        scales[i, :, 0:CYC] = scale[:, i * CYC : (i + 1) * CYC]

    logits[...] = jnp.zeros_like(logits)

    def chunk_step(i, energy):
        pltpu.make_async_copy(refs.at[:, pl.ds(0, WIDE)], raw.at[i], sems.at[0, i]).wait()
        lane_r = lax.broadcasted_iota(jnp.int32, (K_OWN, 128), 1)
        tiles = [raw[i, :, 128 * t : 128 * t + 128] for t in range(TILES)]
        for r2 in range(N2):
            cache = {}
            plans = rolled_plan((SPAN - N1 * HOP * r2) % SPAN)
            for t in range(TILES):
                turned[r2 * KP : r2 * KP + K_OWN, 128 * t : 128 * t + 128] = gather_tile(
                    plans[t], lambda u: tiles[u], lane_r, cache
                )
        lane_e = lax.broadcasted_iota(jnp.int32, (K_OWN, CYCLES), 1)
        sums = [None] * CYC
        for t in range(TILES):
            square = jnp.square(tiles[t].astype(jnp.float32))
            lo, hi = 128 * t // SPAN, (128 * t + 127) // SPAN
            parts = [(lo, square)]
            if hi != lo:
                edge = hi * SPAN - 128 * t
                parts = [
                    (lo, jnp.where(lane_r < edge, square, 0.0)),
                    (hi, jnp.where(lane_r >= edge, square, 0.0)),
                ]
            for c, part in parts:
                sums[c] = part if sums[c] is None else sums[c] + part
        for c in range(CYC):
            total = jnp.sum(sums[c], axis=1, keepdims=True)
            energy = jnp.where(lane_e == i * CYC + c, total, energy)

        pltpu.make_async_copy(images.at[:, pl.ds(0, WIDE)], pix.at[i], sems.at[1, i]).wait()
        for r1 in range(N1):
            stack[i, r1 * QP + READ : (r1 + 1) * QP, :] = jnp.zeros(
                (QP - READ, WIDE), jnp.bfloat16
            )

        def row_step(j, carry):
            rows = pl.ds(pl.multiple_of(j * 16, 16), 16)
            lane_w = lax.broadcasted_iota(jnp.int32, (16, 128), 1)
            factor = scales[i, rows, :]
            cols = [jnp.broadcast_to(factor[:, c : c + 1], (16, 128)) for c in range(CYC)]
            weighted = []
            for t in range(TILES):
                lo, hi = 128 * t // SPAN, (128 * t + 127) // SPAN
                amount = cols[lo]
                if hi != lo:
                    amount = jnp.where(lane_w < hi * SPAN - 128 * t, cols[lo], cols[hi])
                pixels = pix[i, rows, 128 * t : 128 * t + 128].astype(jnp.float32)
                weighted.append((amount * pixels).astype(jnp.bfloat16))
            for r1 in range(N1):
                cache = {}
                plans = rolled_plan(HOP * r1)
                out_rows = pl.ds(pl.multiple_of(r1 * QP + j * 16, 16), 16)
                for t in range(TILES):
                    stack[i, out_rows, 128 * t : 128 * t + 128] = gather_tile(
                        plans[t], lambda u: weighted[u], lane_w, cache
                    )
            return carry

        lax.fori_loop(0, READ // 16, row_step, 0)
        logits[...] += lax.dot_general(
            turned[...], stack[i], (((1,), (1,)), ((), ())), preferred_element_type=jnp.float32
        )
        return energy

    energy = lax.fori_loop(0, CHUNKS, chunk_step, jnp.zeros((K_OWN, CYCLES), jnp.float32))
    ref_power = lax.dot_general(
        energy,
        power,
        (((1,), (1,)), ((), ())),
        precision=HIGH,
        preferred_element_type=jnp.float32,
    )
    half = 0.5 * ref_power
    lane_q = lax.broadcasted_iota(jnp.int32, (K_OWN, QP), 1)
    alive = lane_q < counts[me]
    peak = jnp.full((K_OWN, QP), -3.0e38, jnp.float32)
    for r2 in range(N2):
        for r1 in range(N1):
            rows = slice(r2 * KP, r2 * KP + K_OWN)
            cols = slice(r1 * QP, (r1 + 1) * QP)
            value = jnp.where(alive, logits[rows, cols] - half, 0.0)
            logits[rows, cols] = value
            peak = jnp.maximum(peak, value)
    peak = jnp.max(peak, axis=0, keepdims=True)
    mass = jnp.zeros((K_OWN, QP), jnp.float32)
    prob[...] = jnp.zeros_like(prob)
    for r2 in range(N2):
        for r1 in range(N1):
            rows = slice(r2 * KP, r2 * KP + K_OWN)
            cols = slice(r1 * QP, (r1 + 1) * QP)
            value = jnp.exp(logits[rows, cols] - peak)
            prob[rows, cols] = value
            mass = mass + value
    mass = jnp.sum(mass, axis=0, keepdims=True)
    sub = lax.broadcasted_iota(jnp.int32, (8, QP), 0)
    block = jnp.where(sub == 0, peak, jnp.where(alive[0:1, :], mass, 0.0))
    for i in range(8):
        stats[i] = block


def scatter_chunk(stack, post, dens, partial, out, x_to):
    partial[...] = jnp.dot(post[...], stack[x_to], preferred_element_type=jnp.float32)
    lane = lax.broadcasted_iota(jnp.int32, (KP, 128), 1)
    caches = [{} for _ in range(N2)]
    for c in range(CYC):
        for part in range(4):
            total = None
            for r2 in range(N2):
                value = gather_tile(
                    packed_plan(c, part, N1 * HOP * r2),
                    lambda u: partial[r2 * KP : (r2 + 1) * KP, 128 * u : 128 * u + 128],
                    lane,
                    caches[r2],
                )
                total = value if total is None else total + value
            if part == 3:
                total = jnp.where(lane == EDGE, dens[x_to][:, c : c + 1], total)
                high = pltpu.roll(total[LOW : 2 * LOW], 64, axis=1)
                total = jnp.where(lane[:LOW] < 64, total[:LOW], high)
                out[c, 3 * K_OWN : PACK, :] = total.astype(out.dtype)
            else:
                out[c, K_OWN * part : K_OWN * (part + 1), :] = total[:K_OWN].astype(out.dtype)


def first_chunk_kernel(
    hop, stack, prob, stats, power, out, post, dens, conf, partial
):
    me = lax.axis_index("dom")
    seat = lax.axis_index("cls")
    peak = stats[0][0:1, :]
    for i in range(1, 8):
        peak = jnp.maximum(peak, stats[i][0:1, :])
    mass = jnp.zeros((1, QP), jnp.float32)
    for i in range(8):
        mass = mass + stats[i][1:2, :] * jnp.exp(stats[i][0:1, :] - peak)
    alive = mass > 0.0
    own_peak = stats[seat][0:1, :]
    factor = jnp.where(alive, jnp.exp(own_peak - peak) / mass, 0.0)
    conf[...] = jnp.where(alive, 1.0 / mass, 0.0)[:, :READ]
    total = jnp.zeros((KP, QP), jnp.float32)
    for r2 in range(N2):
        for r1 in range(N1):
            rows = slice(r2 * KP, (r2 + 1) * KP)
            cols = slice(r1 * QP, (r1 + 1) * QP)
            value = prob[rows, cols] * factor
            total = total + value
            post[rows, cols] = value.astype(jnp.bfloat16)
    den = jnp.dot(total, power[...], precision=HIGH, preferred_element_type=jnp.float32)
    for i in range(CHUNKS):
        dens[i, :, 0:CYC] = den[:, i * CYC : (i + 1) * CYC]
    scatter_chunk(stack, post, dens, partial, out, lax.rem(me // Z_SIZE + hop, X_SIZE))


def chunk_kernel(hop, stack, post, dens, out, partial):
    me = lax.axis_index("dom")
    scatter_chunk(stack, post, dens, partial, out, lax.rem(me // Z_SIZE + hop, X_SIZE))


def finish_kernel(pieces, out, acc):
    total = pieces[0].astype(jnp.float32)
    for i in range(1, Z_SIZE):
        total = total + pieces[i].astype(jnp.float32)
    acc[...] = total
    low = acc[3 * K_OWN : PACK, :]
    high = acc[3 * K_OWN : 4 * K_OWN - LOW, 64:128]
    den_low = low[:, EDGE : EDGE + 1] + ridge_term
    den_high = high[:, EDGE : EDGE + 1] + ridge_term
    den = jnp.concatenate([den_low, den_high], axis=0)
    for part in range(3):
        out[:, 128 * part : 128 * (part + 1)] = acc[K_OWN * part : K_OWN * (part + 1), :] / den
    out[0:LOW, 384:SPAN] = low[:, 0:EDGE] / den_low
    out[LOW:K_OWN, 384:SPAN] = high[:, 0:EDGE] / den_high


def in_hbm(x):
    return pltpu.with_memory_space_constraint(x, pltpu.HBM)


def in_vmem(x):
    return pltpu.with_memory_space_constraint(x, pltpu.VMEM)


def body(images, pick_counts, group_of, ctf_table, precision, references):
    f32, bf16 = jnp.float32, jnp.bfloat16
    operands = (
        images,
        references,
        group_of.reshape(24, 128),
        ctf_table,
        precision.reshape(1, CYCLES),
        pick_counts,
    )
    stack, prob, stats, power = pl.pallas_call(
        match_kernel,
        out_shape=(
            pltpu.VMEM((CHUNKS, N1 * QP, WIDE), bf16),
            pltpu.VMEM((N2 * KP, N1 * QP), f32),
            jax.ShapeDtypeStruct((8, 8, QP), f32),
            pltpu.VMEM((QP, CYCLES), f32),
        ),
        in_specs=[FAR] * 6,
        out_specs=(VM, VM, VM, VM),
        scratch_shapes=[
            pltpu.VMEM((CHUNKS, READ, WIDE), bf16),
            pltpu.VMEM((CHUNKS, K_OWN, WIDE), bf16),
            pltpu.VMEM((N2 * KP, WIDE), bf16),
            pltpu.VMEM((CHUNKS, QP, 128), f32),
            pltpu.VMEM((N2 * KP, N1 * QP), f32),
            pltpu.VMEM((24, 128), jnp.int32),
            pltpu.VMEM((GROUPS, CYCLES), f32),
            pltpu.VMEM((1, CYCLES), f32),
            pltpu.SMEM((32,), jnp.int32),
            pltpu.SemaphoreType.DMA((2, CHUNKS)),
            pltpu.SemaphoreType.DMA((4,)),
        ],
        compiler_params=PARAMS,
        name="match",
    )(*map(in_hbm, operands))
    stats = lax.all_to_all(stats, "cls", 0, 0)
    stack, prob, power = in_vmem(stack), in_vmem(prob), in_vmem(power)

    part_shape = (CYC, PACK, 128)
    partial = pltpu.VMEM((N2 * KP, WIDE), f32)
    across, post, dens, conf = pl.pallas_call(
        functools.partial(first_chunk_kernel, 2),
        out_shape=(
            jax.ShapeDtypeStruct(part_shape, bf16),
            pltpu.VMEM((N2 * KP, N1 * QP), bf16),
            pltpu.VMEM((CHUNKS, KP, 128), f32),
            jax.ShapeDtypeStruct((1, READ), f32),
        ),
        in_specs=[VM, VM, VM, VM],
        out_specs=(VM, VM, VM, VM),
        scratch_shapes=[partial],
        compiler_params=PARAMS,
        name="chunk2",
    )(stack, prob, stats, power)
    post, dens = in_vmem(post), in_vmem(dens)

    def moved(piece, hop):
        ring = [(j, (j // Z_SIZE + hop) % X_SIZE * Z_SIZE + j % Z_SIZE) for j in range(32)]
        return lax.ppermute(piece, "dom", ring)

    def chunk_call(hop, dtype):
        return pl.pallas_call(
            functools.partial(chunk_kernel, hop),
            out_shape=jax.ShapeDtypeStruct(part_shape, dtype),
            in_specs=[VM, VM, VM],
            out_specs=VM,
            scratch_shapes=[partial],
            compiler_params=PARAMS,
        )(stack, post, dens)

    got2 = moved(across, 2)
    got1 = moved(chunk_call(1, bf16), 1)
    got3 = moved(chunk_call(3, bf16), 3)
    own = chunk_call(0, f32)
    total = own + got1.astype(f32) + got2.astype(f32) + got3.astype(f32)
    z_groups = [[x * Z_SIZE + z for z in range(Z_SIZE)] for x in range(X_SIZE)]
    pieces = lax.all_to_all(total.astype(bf16), "dom", 0, 0, axis_index_groups=z_groups)
    new_refs = pl.pallas_call(
        finish_kernel,
        out_shape=jax.ShapeDtypeStruct((K_OWN, SPAN), f32),
        in_specs=[VM],
        out_specs=VM,
        scratch_shapes=[pltpu.VMEM((PACK, 128), f32)],
        compiler_params=PARAMS,
        name="finish",
    )(pieces)
    return new_refs, conf.reshape(READ)


def solution(mesh):
    return jax.shard_map(
        body,
        mesh=mesh,
        in_specs=(P("dom", None), P(), P(), P(), P(), P("cls", None)),
        out_specs=(P("cls", "dom"), P("dom")),
        check_vma=False,
    )
```

```python
import functools

import jax
import jax.numpy as jnp
from jax import lax
from jax.experimental import pallas as pl
from jax.experimental.pallas import tpu as pltpu
from jax.sharding import PartitionSpec as P


CYCLES = 32
ANG = 216
STEP = 6
READ = 96
K_OWN = 25
GROUPS = 32

SPAN = 2 * ANG
HOP = 2 * STEP
N1 = 6
N2 = 6
CHUNKS = 4
CYC = 8
WIDE = CYC * SPAN
TILES = WIDE // 128
EDGE = SPAN - 384
QP = 128
KP = 32
LOW = 13
PACK = 3 * K_OWN + LOW

ridge_term = 0.02
HIGH = lax.Precision.HIGHEST
X_SIZE, Z_SIZE = 4, 8

VM = pl.BlockSpec(memory_space=pltpu.VMEM)
FAR = pl.BlockSpec(memory_space=pltpu.HBM)
PARAMS = pltpu.CompilerParams(vmem_limit_bytes=12 * 1024 * 1024)


def plan(sources):
    runs = []
    for lane, src in enumerate(sources):
        if src is None:
            continue
        key = (src // 128, (src - lane) % 128)
        if runs and runs[-1][2] == key and runs[-1][1] == lane:
            runs[-1][1] = lane + 1
        else:
            runs.append([lane, lane + 1, key])
    return sorted(runs, key=lambda run: run[0] - run[1])


def rolled_plan(shift):
    tiles = []
    for tile in range(TILES):
        sources = []
        for lane in range(128):
            cycle, place = divmod(128 * tile + lane, SPAN)
            sources.append(cycle * SPAN + (place + shift) % SPAN)
        tiles.append(plan(sources))
    return tiles


def packed_plan(cycle, part, shift):
    sources = []
    for lane in range(128):
        place = 128 * part + lane
        sources.append(cycle * SPAN + (place + shift) % SPAN if place < SPAN else None)
    return plan(sources)


def lane_mask(first, last, lane, masks):
    if (first, last) not in masks:
        low, high = jnp.asarray(first, lane.dtype), jnp.asarray(last, lane.dtype)
        if first == 0:
            mask = lane < high
        elif last == 128:
            mask = lane >= low
        else:
            mask = (lane >= low) & (lane < high)
        masks[first, last] = mask
    return masks[first, last]


def gather_tile(runs, load, lane, cache, masks):
    value = None
    for first, last, (tile, turn) in runs:
        key = (tile, turn)
        if key not in cache:
            piece = load(tile)
            cache[key] = pltpu.roll(piece, 128 - turn, axis=1) if turn else piece
        piece = cache[key]
        if value is None:
            value = piece
        else:
            value = jnp.where(lane_mask(first, last, lane, masks), piece, value)
    return value


def store_tiles(ref, row_groups, plans, load, lane):
    caches = [{} for _ in row_groups]
    for t in range(0, TILES, 2):
        masks = {}
        for g, rows in enumerate(row_groups):
            values = [
                gather_tile(plans[u], functools.partial(load, g), lane, caches[g], masks)
                for u in range(t, min(t + 2, TILES))
            ]
            wide = jnp.concatenate(values, axis=1) if len(values) > 1 else values[0]
            ref[rows, 128 * t : 128 * t + wide.shape[1]] = wide


def match_kernel(
    images,
    refs,
    groups_far,
    table_far,
    precision_far,
    counts_far,
    stack,
    prob,
    stats,
    power_out,
    pix,
    raw,
    turned,
    scales,
    logits,
    groups,
    table,
    precision,
    counts,
    sems,
    small_sems,
):
    me = lax.axis_index("dom")
    small = [
        pltpu.make_async_copy(src, dst, small_sems.at[n])
        for n, (src, dst) in enumerate(
            (
                (groups_far, groups),
                (table_far, table),
                (precision_far, precision),
                (counts_far, counts),
            )
        )
    ]
    for copy in small:
        copy.start()
    copies = []
    for i in range(CHUNKS):
        span = pl.ds(i * WIDE, WIDE)
        copies.append(pltpu.make_async_copy(refs.at[:, span], raw.at[i], sems.at[0, i]))
        copies.append(pltpu.make_async_copy(images.at[:, span], pix.at[i], sems.at[1, i]))
    for copy in copies:
        copy.start()
    for copy in small:
        copy.wait()

    lane = lax.broadcasted_iota(jnp.int32, (8, QP), 1)
    base = me * READ
    row = base // 128
    off = base - row * 128
    turn = lax.rem(128 - off, 128)
    head = jnp.broadcast_to(groups[pl.ds(row, 1), :], (8, QP))
    tail = jnp.broadcast_to(groups[pl.ds(jnp.minimum(row + 1, 23), 1), :], (8, QP))
    mine = jnp.where(
        lane + off < 128, pltpu.roll(head, turn, axis=1), pltpu.roll(tail, turn, axis=1)
    )
    hot = (lax.broadcasted_iota(jnp.int32, (QP, QP), 0) == mine[0:1, :]).astype(jnp.float32)
    hot = hot.T[:, :GROUPS]
    ctf = jnp.dot(hot, table[...], precision=HIGH, preferred_element_type=jnp.float32)
    scale = precision[...] * ctf
    power = precision[...] * jnp.square(ctf)
    power_out[...] = power
    for i in range(CHUNKS):
        scales[i, :, 0:CYC] = scale[:, i * CYC : (i + 1) * CYC]

    lane_r = lax.broadcasted_iota(jnp.int32, (K_OWN, 128), 1)
    lane_e = lax.broadcasted_iota(jnp.int32, (K_OWN, CYCLES), 1)
    lane_w = lax.broadcasted_iota(jnp.int32, (16, 128), 1)
    nought = [jnp.minimum(counts[i], 0) for i in range(CHUNKS)]

    def turn_refs(i, energy):
        copies[2 * i].wait()
        tiles = [raw[i, :, 128 * t : 128 * t + 128] for t in range(TILES)]
        lane16 = (lane_r + nought[i]).astype(jnp.int16)
        for r2 in range(N2):
            plans = rolled_plan((SPAN - N1 * HOP * r2) % SPAN)
            rows = [slice(r2 * KP, r2 * KP + K_OWN)]
            store_tiles(turned.at[i % 2], rows, plans, lambda g, u: tiles[u], lane16)
        sums = [None] * CYC
        for t in range(TILES):
            square = jnp.square(tiles[t].astype(jnp.float32))
            lo, hi = 128 * t // SPAN, (128 * t + 127) // SPAN
            parts = [(lo, square)]
            if hi != lo:
                edge = hi * SPAN - 128 * t
                parts = [
                    (lo, jnp.where(lane_r < edge, square, 0.0)),
                    (hi, jnp.where(lane_r >= edge, square, 0.0)),
                ]
            for c, part in parts:
                sums[c] = part if sums[c] is None else sums[c] + part
        for c in range(CYC):
            total = jnp.sum(sums[c], axis=1, keepdims=True)
            energy = jnp.where(lane_e == i * CYC + c, total, energy)
        return energy

    def weigh_images(i):
        copies[2 * i + 1].wait()
        for j in range(READ // 16):
            rows = slice(16 * j, 16 * j + 16)
            factor = scales[i, rows, :]
            cols = [jnp.broadcast_to(factor[:, c : c + 1], (16, 128)) for c in range(CYC)]
            weighted = []
            for t in range(TILES):
                lo, hi = 128 * t // SPAN, (128 * t + 127) // SPAN
                amount = cols[lo]
                if hi != lo:
                    amount = jnp.where(lane_w < hi * SPAN - 128 * t, cols[lo], cols[hi])
                pixels = pix[i, rows, 128 * t : 128 * t + 128].astype(jnp.float32)
                weighted.append((amount * pixels).astype(jnp.bfloat16))
            stack[i, rows, :] = jnp.concatenate(weighted, axis=1)

    def turn_images(i, r1):
        lane16 = (lane_w + nought[i]).astype(jnp.int16)
        groups_in = [slice(16 * j, 16 * j + 16) for j in range(READ // 16)]
        groups_out = [
            slice(r1 * QP + 16 * j, r1 * QP + 16 * j + 16) for j in range(READ // 16)
        ]
        store_tiles(
            stack.at[i],
            groups_out,
            rolled_plan(HOP * r1),
            lambda g, u: stack[i, groups_in[g], 128 * u : 128 * u + 128],
            lane16,
        )

    def multiply(i, part):
        cols = slice(2 * QP * part, 2 * QP * (part + 1))
        value = None
        for span in (slice(0, 14 * 128), slice(14 * 128, WIDE)):
            piece = lax.dot_general(
                turned[i % 2, :, span],
                stack[i, cols, span],
                (((1,), (1,)), ((), ())),
                preferred_element_type=jnp.float32,
            )
            value = piece if value is None else value + piece
        if i:
            value = value + logits[:, cols]
        logits[:, cols] = value

    energy = jnp.zeros((K_OWN, CYCLES), jnp.float32)
    for i in range(CHUNKS):
        for r1 in range(N1):
            stack[i, r1 * QP + READ : (r1 + 1) * QP, :] = jnp.zeros(
                (QP - READ, WIDE), jnp.bfloat16
            )
        energy = turn_refs(i, energy)
        if i:
            multiply(i - 1, 0)
        weigh_images(i)
        for r1 in range(1, N1):
            if i and r1 in (2, 4):
                multiply(i - 1, r1 // 2)
            turn_images(i, r1)
    for part in range(3):
        multiply(CHUNKS - 1, part)

    ref_power = lax.dot_general(
        energy,
        power,
        (((1,), (1,)), ((), ())),
        precision=HIGH,
        preferred_element_type=jnp.float32,
    )
    half = 0.5 * ref_power
    lane_q = lax.broadcasted_iota(jnp.int32, (K_OWN, QP), 1)
    alive = lane_q < counts[me]
    peak = jnp.full((K_OWN, QP), -3.0e38, jnp.float32)
    for r2 in range(N2):
        for r1 in range(N1):
            rows = slice(r2 * KP, r2 * KP + K_OWN)
            cols = slice(r1 * QP, (r1 + 1) * QP)
            value = jnp.where(alive, logits[rows, cols] - half, 0.0)
            logits[rows, cols] = value
            peak = jnp.maximum(peak, value)
    peak = jnp.max(peak, axis=0, keepdims=True)
    mass = jnp.zeros((K_OWN, QP), jnp.float32)
    prob[...] = jnp.zeros_like(prob)
    for r2 in range(N2):
        for r1 in range(N1):
            rows = slice(r2 * KP, r2 * KP + K_OWN)
            cols = slice(r1 * QP, (r1 + 1) * QP)
            value = jnp.exp(logits[rows, cols] - peak)
            prob[rows, cols] = value
            mass = mass + value
    mass = jnp.sum(mass, axis=0, keepdims=True)
    sub = lax.broadcasted_iota(jnp.int32, (8, QP), 0)
    block = jnp.where(sub == 0, peak, jnp.where(alive[0:1, :], mass, 0.0))
    for i in range(8):
        stats[i] = block


def scatter_chunk(stack, post, dens, partial, out, x_to):
    partial[...] = jnp.dot(post[...], stack[x_to], preferred_element_type=jnp.float32)
    lane = lax.broadcasted_iota(jnp.int32, (KP, 128), 1)
    caches = [{} for _ in range(N2)]
    for c in range(CYC):
        for part in range(4):
            total = None
            masks = {}
            for r2 in range(N2):
                value = gather_tile(
                    packed_plan(c, part, N1 * HOP * r2),
                    lambda u: partial[r2 * KP : (r2 + 1) * KP, 128 * u : 128 * u + 128],
                    lane,
                    caches[r2],
                    masks,
                )
                total = value if total is None else total + value
            if part == 3:
                total = jnp.where(lane == EDGE, dens[x_to][:, c : c + 1], total)
                high = pltpu.roll(total[LOW : 2 * LOW], 64, axis=1)
                total = jnp.where(lane[:LOW] < 64, total[:LOW], high)
                out[c, 3 * K_OWN : PACK, :] = total.astype(out.dtype)
            else:
                out[c, K_OWN * part : K_OWN * (part + 1), :] = total[:K_OWN].astype(out.dtype)


def first_chunk_kernel(
    hop, stack, prob, stats, power, out, post, dens, conf, partial
):
    me = lax.axis_index("dom")
    seat = lax.axis_index("cls")
    peak = stats[0][0:1, :]
    for i in range(1, 8):
        peak = jnp.maximum(peak, stats[i][0:1, :])
    mass = jnp.zeros((1, QP), jnp.float32)
    for i in range(8):
        mass = mass + stats[i][1:2, :] * jnp.exp(stats[i][0:1, :] - peak)
    alive = mass > 0.0
    own_peak = stats[seat][0:1, :]
    factor = jnp.where(alive, jnp.exp(own_peak - peak) / mass, 0.0)
    conf[...] = jnp.where(alive, 1.0 / mass, 0.0)[:, :READ]
    total = jnp.zeros((KP, QP), jnp.float32)
    for r2 in range(N2):
        for r1 in range(N1):
            rows = slice(r2 * KP, (r2 + 1) * KP)
            cols = slice(r1 * QP, (r1 + 1) * QP)
            value = prob[rows, cols] * factor
            total = total + value
            post[rows, cols] = value.astype(jnp.bfloat16)
    den = jnp.dot(total, power[...], precision=HIGH, preferred_element_type=jnp.float32)
    for i in range(CHUNKS):
        dens[i, :, 0:CYC] = den[:, i * CYC : (i + 1) * CYC]
    scatter_chunk(stack, post, dens, partial, out, lax.rem(me // Z_SIZE + hop, X_SIZE))


def chunk_kernel(hop, stack, post, dens, out, partial):
    me = lax.axis_index("dom")
    scatter_chunk(stack, post, dens, partial, out, lax.rem(me // Z_SIZE + hop, X_SIZE))


def finish_kernel(pieces, out, acc):
    total = pieces[0].astype(jnp.float32)
    for i in range(1, Z_SIZE):
        total = total + pieces[i].astype(jnp.float32)
    acc[...] = total
    low = acc[3 * K_OWN : PACK, :]
    high = acc[3 * K_OWN : 4 * K_OWN - LOW, 64:128]
    den_low = low[:, EDGE : EDGE + 1] + ridge_term
    den_high = high[:, EDGE : EDGE + 1] + ridge_term
    den = jnp.concatenate([den_low, den_high], axis=0)
    for part in range(3):
        out[:, 128 * part : 128 * (part + 1)] = acc[K_OWN * part : K_OWN * (part + 1), :] / den
    out[0:LOW, 384:SPAN] = low[:, 0:EDGE] / den_low
    out[LOW:K_OWN, 384:SPAN] = high[:, 0:EDGE] / den_high


def in_hbm(x):
    return pltpu.with_memory_space_constraint(x, pltpu.HBM)


def in_vmem(x):
    return pltpu.with_memory_space_constraint(x, pltpu.VMEM)


def body(images, pick_counts, group_of, ctf_table, precision, references):
    f32, bf16 = jnp.float32, jnp.bfloat16
    operands = (
        images,
        references,
        group_of.reshape(24, 128),
        ctf_table,
        precision.reshape(1, CYCLES),
        pick_counts,
    )
    stack, prob, stats, power = pl.pallas_call(
        match_kernel,
        out_shape=(
            pltpu.VMEM((CHUNKS, N1 * QP, WIDE), bf16),
            pltpu.VMEM((N2 * KP, N1 * QP), f32),
            jax.ShapeDtypeStruct((8, 8, QP), f32),
            pltpu.VMEM((QP, CYCLES), f32),
        ),
        in_specs=[FAR] * 6,
        out_specs=(VM, VM, VM, VM),
        scratch_shapes=[
            pltpu.VMEM((CHUNKS, READ, WIDE), bf16),
            pltpu.VMEM((CHUNKS, K_OWN, WIDE), bf16),
            pltpu.VMEM((2, N2 * KP, WIDE), bf16),
            pltpu.VMEM((CHUNKS, QP, 128), f32),
            pltpu.VMEM((N2 * KP, N1 * QP), f32),
            pltpu.VMEM((24, 128), jnp.int32),
            pltpu.VMEM((GROUPS, CYCLES), f32),
            pltpu.VMEM((1, CYCLES), f32),
            pltpu.SMEM((32,), jnp.int32),
            pltpu.SemaphoreType.DMA((2, CHUNKS)),
            pltpu.SemaphoreType.DMA((4,)),
        ],
        compiler_params=PARAMS,
        name="match",
    )(*map(in_hbm, operands))
    stats = lax.all_to_all(stats, "cls", 0, 0)
    stack, prob, power = in_vmem(stack), in_vmem(prob), in_vmem(power)

    part_shape = (CYC, PACK, 128)
    partial = pltpu.VMEM((N2 * KP, WIDE), f32)
    across, post, dens, conf = pl.pallas_call(
        functools.partial(first_chunk_kernel, 2),
        out_shape=(
            jax.ShapeDtypeStruct(part_shape, bf16),
            pltpu.VMEM((N2 * KP, N1 * QP), bf16),
            pltpu.VMEM((CHUNKS, KP, 128), f32),
            jax.ShapeDtypeStruct((1, READ), f32),
        ),
        in_specs=[VM, VM, VM, VM],
        out_specs=(VM, VM, VM, VM),
        scratch_shapes=[partial],
        compiler_params=PARAMS,
        name="chunk2",
    )(stack, prob, stats, power)
    post, dens = in_vmem(post), in_vmem(dens)

    def moved(piece, hop):
        ring = [(j, (j // Z_SIZE + hop) % X_SIZE * Z_SIZE + j % Z_SIZE) for j in range(32)]
        return lax.ppermute(piece, "dom", ring)

    def chunk_call(hop, dtype):
        return pl.pallas_call(
            functools.partial(chunk_kernel, hop),
            out_shape=jax.ShapeDtypeStruct(part_shape, dtype),
            in_specs=[VM, VM, VM],
            out_specs=VM,
            scratch_shapes=[partial],
            compiler_params=PARAMS,
        )(stack, post, dens)

    got2 = moved(across, 2)
    got1 = moved(chunk_call(1, bf16), 1)
    got3 = moved(chunk_call(3, bf16), 3)
    own = chunk_call(0, f32)
    total = own + got1.astype(f32) + got2.astype(f32) + got3.astype(f32)
    z_groups = [[x * Z_SIZE + z for z in range(Z_SIZE)] for x in range(X_SIZE)]
    pieces = lax.all_to_all(total.astype(bf16), "dom", 0, 0, axis_index_groups=z_groups)
    new_refs = pl.pallas_call(
        finish_kernel,
        out_shape=jax.ShapeDtypeStruct((K_OWN, SPAN), f32),
        in_specs=[VM],
        out_specs=VM,
        scratch_shapes=[pltpu.VMEM((PACK, 128), f32)],
        compiler_params=PARAMS,
        name="finish",
    )(pieces)
    return new_refs, conf.reshape(READ)


def solution(mesh):
    return jax.shard_map(
        body,
        mesh=mesh,
        in_specs=(P("dom", None), P(), P(), P(), P(), P("cls", None)),
        out_specs=(P("cls", "dom"), P("dom")),
        check_vma=False,
    )
```

```python
import functools

import jax
import jax.numpy as jnp
from jax import lax
from jax.experimental import pallas as pl
from jax.experimental.pallas import tpu as pltpu
from jax.sharding import PartitionSpec as P


CYCLES = 32
ANG = 216
STEP = 6
READ = 96
K_OWN = 25
GROUPS = 32

SPAN = 2 * ANG
HOP = 2 * STEP
N1 = 6
N2 = 6
CHUNKS = 4
CYC = 8
WIDE = CYC * SPAN
TILES = WIDE // 128
EDGE = SPAN - 384
QP = 128
KP = 32
LOW = 13
PACK = 3 * K_OWN + LOW

ridge_term = 0.02
HIGH = lax.Precision.HIGHEST
X_SIZE, Z_SIZE = 4, 8

VM = pl.BlockSpec(memory_space=pltpu.VMEM)
FAR = pl.BlockSpec(memory_space=pltpu.HBM)
PARAMS = pltpu.CompilerParams(vmem_limit_bytes=12 * 1024 * 1024)


def plan(sources):
    runs = []
    for lane, src in enumerate(sources):
        if src is None:
            continue
        key = (src // 128, (src - lane) % 128)
        if runs and runs[-1][2] == key and runs[-1][1] == lane:
            runs[-1][1] = lane + 1
        else:
            runs.append([lane, lane + 1, key])
    return sorted(runs, key=lambda run: run[0] - run[1])


def rolled_plan(shift):
    tiles = []
    for tile in range(TILES):
        sources = []
        for lane in range(128):
            cycle, place = divmod(128 * tile + lane, SPAN)
            sources.append(cycle * SPAN + (place + shift) % SPAN)
        tiles.append(plan(sources))
    return tiles


def packed_plan(cycle, part, shift):
    sources = []
    for lane in range(128):
        place = 128 * part + lane
        sources.append(cycle * SPAN + (place + shift) % SPAN if place < SPAN else None)
    return plan(sources)


def lane_mask(first, last, lane, masks):
    if (first, last) not in masks:
        low, high = jnp.asarray(first, lane.dtype), jnp.asarray(last, lane.dtype)
        if first == 0:
            mask = lane < high
        elif last == 128:
            mask = lane >= low
        else:
            mask = (lane >= low) & (lane < high)
        masks[first, last] = mask
    return masks[first, last]


def gather_tile(runs, load, lane, cache, masks):
    value = None
    for first, last, (tile, turn) in runs:
        key = (tile, turn)
        if key not in cache:
            piece = load(tile)
            cache[key] = pltpu.roll(piece, 128 - turn, axis=1) if turn else piece
        piece = cache[key]
        if value is None:
            value = piece
        else:
            value = jnp.where(lane_mask(first, last, lane, masks), piece, value)
    return value


def store_tiles(ref, row_groups, plans, load, lane):
    caches = [{} for _ in row_groups]
    for t in range(0, TILES, 2):
        masks = {}
        for g, rows in enumerate(row_groups):
            values = [
                gather_tile(plans[u], functools.partial(load, g), lane, caches[g], masks)
                for u in range(t, min(t + 2, TILES))
            ]
            wide = jnp.concatenate(values, axis=1) if len(values) > 1 else values[0]
            ref[rows, 128 * t : 128 * t + wide.shape[1]] = wide


def match_kernel(
    images,
    refs,
    groups_far,
    table_far,
    precision_far,
    counts_far,
    stack,
    prob,
    stats,
    power_out,
    pix,
    raw,
    turned,
    scales,
    logits,
    groups,
    table,
    precision,
    counts,
    sems,
    small_sems,
):
    me = lax.axis_index("dom")
    small = [
        pltpu.make_async_copy(src, dst, small_sems.at[n])
        for n, (src, dst) in enumerate(
            (
                (groups_far, groups),
                (table_far, table),
                (precision_far, precision),
                (counts_far, counts),
            )
        )
    ]
    copies = []
    for i in range(CHUNKS):
        span = pl.ds(i * WIDE, WIDE)
        copies.append(pltpu.make_async_copy(refs.at[:, span], raw.at[i], sems.at[0, i]))
        copies.append(pltpu.make_async_copy(images.at[:, span], pix.at[i], sems.at[1, i]))
    small[3].start()
    copies[0].start()
    for copy in small[:3] + copies[1:]:
        copy.start()
    small[3].wait()

    lane_r = lax.broadcasted_iota(jnp.int32, (K_OWN, 128), 1)
    lane_e = lax.broadcasted_iota(jnp.int32, (K_OWN, CYCLES), 1)
    lane_w = lax.broadcasted_iota(jnp.int32, (16, 128), 1)
    nought = [jnp.minimum(counts[i], 0) for i in range(CHUNKS)]

    def turn_refs(i, energy):
        copies[2 * i].wait()
        tiles = [raw[i, :, 128 * t : 128 * t + 128] for t in range(TILES)]
        lane16 = (lane_r + nought[i]).astype(jnp.int16)
        for r2 in range(N2):
            plans = rolled_plan((SPAN - N1 * HOP * r2) % SPAN)
            rows = [slice(r2 * KP, r2 * KP + K_OWN)]
            store_tiles(turned.at[i % 2], rows, plans, lambda g, u: tiles[u], lane16)
        sums = [None] * CYC
        for t in range(TILES):
            square = jnp.square(tiles[t].astype(jnp.float32))
            lo, hi = 128 * t // SPAN, (128 * t + 127) // SPAN
            parts = [(lo, square)]
            if hi != lo:
                edge = hi * SPAN - 128 * t
                parts = [
                    (lo, jnp.where(lane_r < edge, square, 0.0)),
                    (hi, jnp.where(lane_r >= edge, square, 0.0)),
                ]
            for c, part in parts:
                sums[c] = part if sums[c] is None else sums[c] + part
        for c in range(CYC):
            total = jnp.sum(sums[c], axis=1, keepdims=True)
            energy = jnp.where(lane_e == i * CYC + c, total, energy)
        return energy

    def weigh_images(i):
        copies[2 * i + 1].wait()
        for j in range(READ // 16):
            rows = slice(16 * j, 16 * j + 16)
            factor = scales[i, rows, :]
            cols = [jnp.broadcast_to(factor[:, c : c + 1], (16, 128)) for c in range(CYC)]
            weighted = []
            for t in range(TILES):
                lo, hi = 128 * t // SPAN, (128 * t + 127) // SPAN
                amount = cols[lo]
                if hi != lo:
                    amount = jnp.where(lane_w < hi * SPAN - 128 * t, cols[lo], cols[hi])
                pixels = pix[i, rows, 128 * t : 128 * t + 128].astype(jnp.float32)
                weighted.append((amount * pixels).astype(jnp.bfloat16))
            stack[i, rows, :] = jnp.concatenate(weighted, axis=1)

    def turn_images(i, r1):
        lane16 = (lane_w + nought[i]).astype(jnp.int16)
        groups_in = [slice(16 * j, 16 * j + 16) for j in range(READ // 16)]
        groups_out = [
            slice(r1 * QP + 16 * j, r1 * QP + 16 * j + 16) for j in range(READ // 16)
        ]
        store_tiles(
            stack.at[i],
            groups_out,
            rolled_plan(HOP * r1),
            lambda g, u: stack[i, groups_in[g], 128 * u : 128 * u + 128],
            lane16,
        )

    def multiply(i, part):
        cols = slice(2 * QP * part, 2 * QP * (part + 1))
        value = None
        for span in (slice(0, 14 * 128), slice(14 * 128, WIDE)):
            piece = lax.dot_general(
                turned[i % 2, :, span],
                stack[i, cols, span],
                (((1,), (1,)), ((), ())),
                preferred_element_type=jnp.float32,
            )
            value = piece if value is None else value + piece
        if i:
            value = value + logits[:, cols]
        logits[:, cols] = value

    energy = turn_refs(0, jnp.zeros((K_OWN, CYCLES), jnp.float32))
    for copy in small[:3]:
        copy.wait()
    lane = lax.broadcasted_iota(jnp.int32, (8, QP), 1)
    base = me * READ
    row = base // 128
    off = base - row * 128
    turn = lax.rem(128 - off, 128)
    head = jnp.broadcast_to(groups[pl.ds(row, 1), :], (8, QP))
    tail = jnp.broadcast_to(groups[pl.ds(jnp.minimum(row + 1, 23), 1), :], (8, QP))
    mine = jnp.where(
        lane + off < 128, pltpu.roll(head, turn, axis=1), pltpu.roll(tail, turn, axis=1)
    )
    hot = (lax.broadcasted_iota(jnp.int32, (QP, QP), 0) == mine[0:1, :]).astype(jnp.float32)
    hot = hot.T[:, :GROUPS]
    ctf = jnp.dot(hot, table[...], precision=HIGH, preferred_element_type=jnp.float32)
    scale = precision[...] * ctf
    power = precision[...] * jnp.square(ctf)
    power_out[...] = power
    for i in range(CHUNKS):
        scales[i, :, 0:CYC] = scale[:, i * CYC : (i + 1) * CYC]

    for i in range(CHUNKS):
        if i:
            energy = turn_refs(i, energy)
            multiply(i - 1, 0)
        weigh_images(i)
        for r1 in range(1, N1):
            if i and r1 in (2, 4):
                multiply(i - 1, r1 // 2)
            turn_images(i, r1)
    for part in range(3):
        multiply(CHUNKS - 1, part)

    ref_power = lax.dot_general(
        energy,
        power,
        (((1,), (1,)), ((), ())),
        precision=HIGH,
        preferred_element_type=jnp.float32,
    )
    half = 0.5 * ref_power
    lane_q = lax.broadcasted_iota(jnp.int32, (K_OWN, QP), 1)
    alive = lane_q < counts[me]
    peak = jnp.full((K_OWN, QP), -3.0e38, jnp.float32)
    for r2 in range(N2):
        for r1 in range(N1):
            rows = slice(r2 * KP, r2 * KP + K_OWN)
            cols = slice(r1 * QP, (r1 + 1) * QP)
            value = jnp.where(alive, logits[rows, cols] - half, 0.0)
            logits[rows, cols] = value
            peak = jnp.maximum(peak, value)
    peak = jnp.max(peak, axis=0, keepdims=True)
    mass = jnp.zeros((K_OWN, QP), jnp.float32)
    prob[...] = jnp.zeros_like(prob)
    for r2 in range(N2):
        for r1 in range(N1):
            rows = slice(r2 * KP, r2 * KP + K_OWN)
            cols = slice(r1 * QP, (r1 + 1) * QP)
            value = jnp.exp(logits[rows, cols] - peak)
            prob[rows, cols] = value
            mass = mass + value
    mass = jnp.sum(mass, axis=0, keepdims=True)
    sub = lax.broadcasted_iota(jnp.int32, (8, QP), 0)
    block = jnp.where(sub == 0, peak, jnp.where(alive[0:1, :], mass, 0.0))
    for i in range(8):
        stats[i] = block


def scatter_chunk(stack, post, dens, partial, out, x_to):
    rows = [stack[x_to, r1 * QP : r1 * QP + READ, :] for r1 in range(N1)]
    partial[...] = jnp.dot(
        post[...], jnp.concatenate(rows, axis=0), preferred_element_type=jnp.float32
    )
    lane = lax.broadcasted_iota(jnp.int32, (KP, 128), 1)
    caches = [{} for _ in range(N2)]
    for c in range(CYC):
        for part in range(4):
            total = None
            masks = {}
            for r2 in range(N2):
                value = gather_tile(
                    packed_plan(c, part, N1 * HOP * r2),
                    lambda u: partial[r2 * KP : (r2 + 1) * KP, 128 * u : 128 * u + 128],
                    lane,
                    caches[r2],
                    masks,
                )
                total = value if total is None else total + value
            if part == 3:
                total = jnp.where(lane == EDGE, dens[x_to][:, c : c + 1], total)
                high = pltpu.roll(total[LOW : 2 * LOW], 64, axis=1)
                total = jnp.where(lane[:LOW] < 64, total[:LOW], high)
                out[c, 3 * K_OWN : PACK, :] = total.astype(out.dtype)
            else:
                out[c, K_OWN * part : K_OWN * (part + 1), :] = total[:K_OWN].astype(out.dtype)


def first_chunk_kernel(
    hop, stack, prob, stats, power, out, post, dens, conf, partial
):
    me = lax.axis_index("dom")
    seat = lax.axis_index("cls")
    peak = stats[0][0:1, :]
    for i in range(1, 8):
        peak = jnp.maximum(peak, stats[i][0:1, :])
    mass = jnp.zeros((1, QP), jnp.float32)
    for i in range(8):
        mass = mass + stats[i][1:2, :] * jnp.exp(stats[i][0:1, :] - peak)
    alive = mass > 0.0
    own_peak = stats[seat][0:1, :]
    factor = jnp.where(alive, jnp.exp(own_peak - peak) / mass, 0.0)
    conf[...] = jnp.where(alive, 1.0 / mass, 0.0)[:, :READ]
    total = jnp.zeros((KP, QP), jnp.float32)
    for r2 in range(N2):
        for r1 in range(N1):
            rows = slice(r2 * KP, (r2 + 1) * KP)
            cols = slice(r1 * QP, (r1 + 1) * QP)
            value = prob[rows, cols] * factor
            total = total + value
            post[rows, r1 * READ : (r1 + 1) * READ] = value[:, :READ].astype(jnp.bfloat16)
    den = jnp.dot(total, power[...], precision=HIGH, preferred_element_type=jnp.float32)
    for i in range(CHUNKS):
        dens[i, :, 0:CYC] = den[:, i * CYC : (i + 1) * CYC]
    scatter_chunk(stack, post, dens, partial, out, lax.rem(me // Z_SIZE + hop, X_SIZE))


def chunk_kernel(hop, stack, post, dens, out, partial):
    me = lax.axis_index("dom")
    scatter_chunk(stack, post, dens, partial, out, lax.rem(me // Z_SIZE + hop, X_SIZE))


def finish_kernel(pieces, out, acc):
    total = pieces[0].astype(jnp.float32)
    for i in range(1, Z_SIZE):
        total = total + pieces[i].astype(jnp.float32)
    acc[...] = total
    low = acc[3 * K_OWN : PACK, :]
    high = acc[3 * K_OWN : 4 * K_OWN - LOW, 64:128]
    den_low = low[:, EDGE : EDGE + 1] + ridge_term
    den_high = high[:, EDGE : EDGE + 1] + ridge_term
    den = jnp.concatenate([den_low, den_high], axis=0)
    for part in range(3):
        out[:, 128 * part : 128 * (part + 1)] = acc[K_OWN * part : K_OWN * (part + 1), :] / den
    out[0:LOW, 384:SPAN] = low[:, 0:EDGE] / den_low
    out[LOW:K_OWN, 384:SPAN] = high[:, 0:EDGE] / den_high


def in_hbm(x):
    return pltpu.with_memory_space_constraint(x, pltpu.HBM)


def in_vmem(x):
    return pltpu.with_memory_space_constraint(x, pltpu.VMEM)


def body(images, pick_counts, group_of, ctf_table, precision, references):
    f32, bf16 = jnp.float32, jnp.bfloat16
    operands = (
        images,
        references,
        group_of.reshape(24, 128),
        ctf_table,
        precision.reshape(1, CYCLES),
        pick_counts,
    )
    stack, prob, stats, power = pl.pallas_call(
        match_kernel,
        out_shape=(
            pltpu.VMEM((CHUNKS, N1 * QP, WIDE), bf16),
            pltpu.VMEM((N2 * KP, N1 * QP), f32),
            jax.ShapeDtypeStruct((8, 8, QP), f32),
            pltpu.VMEM((QP, CYCLES), f32),
        ),
        in_specs=[FAR] * 6,
        out_specs=(VM, VM, VM, VM),
        scratch_shapes=[
            pltpu.VMEM((CHUNKS, READ, WIDE), bf16),
            pltpu.VMEM((CHUNKS, K_OWN, WIDE), bf16),
            pltpu.VMEM((2, N2 * KP, WIDE), bf16),
            pltpu.VMEM((CHUNKS, QP, 128), f32),
            pltpu.VMEM((N2 * KP, N1 * QP), f32),
            pltpu.VMEM((24, 128), jnp.int32),
            pltpu.VMEM((GROUPS, CYCLES), f32),
            pltpu.VMEM((1, CYCLES), f32),
            pltpu.SMEM((32,), jnp.int32),
            pltpu.SemaphoreType.DMA((2, CHUNKS)),
            pltpu.SemaphoreType.DMA((4,)),
        ],
        compiler_params=PARAMS,
        name="match",
    )(*map(in_hbm, operands))
    stats = lax.all_to_all(stats, "cls", 0, 0)
    stack, prob, power = in_vmem(stack), in_vmem(prob), in_vmem(power)

    part_shape = (CYC, PACK, 128)
    partial = pltpu.VMEM((N2 * KP, WIDE), f32)
    across, post, dens, conf = pl.pallas_call(
        functools.partial(first_chunk_kernel, 2),
        out_shape=(
            jax.ShapeDtypeStruct(part_shape, bf16),
            pltpu.VMEM((N2 * KP, N1 * READ), bf16),
            pltpu.VMEM((CHUNKS, KP, 128), f32),
            jax.ShapeDtypeStruct((1, READ), f32),
        ),
        in_specs=[VM, VM, VM, VM],
        out_specs=(VM, VM, VM, VM),
        scratch_shapes=[partial],
        compiler_params=PARAMS,
        name="chunk2",
    )(stack, prob, stats, power)
    post, dens = in_vmem(post), in_vmem(dens)

    def moved(piece, hop):
        ring = [(j, (j // Z_SIZE + hop) % X_SIZE * Z_SIZE + j % Z_SIZE) for j in range(32)]
        return lax.ppermute(piece, "dom", ring)

    def chunk_call(hop, dtype):
        return pl.pallas_call(
            functools.partial(chunk_kernel, hop),
            out_shape=jax.ShapeDtypeStruct(part_shape, dtype),
            in_specs=[VM, VM, VM],
            out_specs=VM,
            scratch_shapes=[partial],
            compiler_params=PARAMS,
        )(stack, post, dens)

    got2 = moved(across, 2)
    got1 = moved(chunk_call(1, bf16), 1)
    got3 = moved(chunk_call(3, bf16), 3)
    own = chunk_call(0, f32)
    total = own + got1.astype(f32) + got2.astype(f32) + got3.astype(f32)
    z_groups = [[x * Z_SIZE + z for z in range(Z_SIZE)] for x in range(X_SIZE)]
    pieces = lax.all_to_all(total.astype(bf16), "dom", 0, 0, axis_index_groups=z_groups)
    new_refs = pl.pallas_call(
        finish_kernel,
        out_shape=jax.ShapeDtypeStruct((K_OWN, SPAN), f32),
        in_specs=[VM],
        out_specs=VM,
        scratch_shapes=[pltpu.VMEM((PACK, 128), f32)],
        compiler_params=PARAMS,
        name="finish",
    )(pieces)
    return new_refs, conf.reshape(READ)


def solution(mesh):
    return jax.shard_map(
        body,
        mesh=mesh,
        in_specs=(P("dom", None), P(), P(), P(), P(), P("cls", None)),
        out_specs=(P("cls", "dom"), P("dom")),
        check_vma=False,
    )
```

```python
import functools

import jax
import jax.numpy as jnp
from jax import lax
from jax.experimental import pallas as pl
from jax.experimental.pallas import tpu as pltpu
from jax.sharding import PartitionSpec as P


CYCLES = 32
ANG = 216
STEP = 6
READ = 96
K_OWN = 25
GROUPS = 32

SPAN = 2 * ANG
HOP = 2 * STEP
N1 = 6
N2 = 6
CHUNKS = 4
CYC = 8
WIDE = CYC * SPAN
TILES = WIDE // 128
EDGE = SPAN - 384
QP = 128
KP = 32
LOW = 13
PACK = 3 * K_OWN + LOW

ridge_term = 0.02
HIGH = lax.Precision.HIGHEST
X_SIZE, Z_SIZE = 4, 8

VM = pl.BlockSpec(memory_space=pltpu.VMEM)
FAR = pl.BlockSpec(memory_space=pltpu.HBM)
PARAMS = pltpu.CompilerParams(vmem_limit_bytes=12 * 1024 * 1024)


def plan(sources):
    runs = []
    for lane, src in enumerate(sources):
        if src is None:
            continue
        key = (src // 128, (src - lane) % 128)
        if runs and runs[-1][2] == key and runs[-1][1] == lane:
            runs[-1][1] = lane + 1
        else:
            runs.append([lane, lane + 1, key])
    return sorted(runs, key=lambda run: run[0] - run[1])


def rolled_plan(shift):
    tiles = []
    for tile in range(TILES):
        sources = []
        for lane in range(128):
            cycle, place = divmod(128 * tile + lane, SPAN)
            sources.append(cycle * SPAN + (place + shift) % SPAN)
        tiles.append(plan(sources))
    return tiles


def packed_plan(cycle, part, shift):
    sources = []
    for lane in range(128):
        place = 128 * part + lane
        sources.append(cycle * SPAN + (place + shift) % SPAN if place < SPAN else None)
    return plan(sources)


def lane_mask(first, last, lane, masks):
    if (first, last) not in masks:
        low, high = jnp.asarray(first, lane.dtype), jnp.asarray(last, lane.dtype)
        if first == 0:
            mask = lane < high
        elif last == 128:
            mask = lane >= low
        else:
            mask = (lane >= low) & (lane < high)
        masks[first, last] = mask
    return masks[first, last]


def gather_tile(runs, load, lane, cache, masks):
    value = None
    for first, last, (tile, turn) in runs:
        key = (tile, turn)
        if key not in cache:
            piece = load(tile)
            cache[key] = pltpu.roll(piece, 128 - turn, axis=1) if turn else piece
        piece = cache[key]
        if value is None:
            value = piece
        else:
            value = jnp.where(lane_mask(first, last, lane, masks), piece, value)
    return value


def store_tiles(ref, row_groups, plans, load, lane):
    caches = [{} for _ in row_groups]
    for t in range(0, TILES, 2):
        masks = {}
        for g, rows in enumerate(row_groups):
            values = [
                gather_tile(plans[u], functools.partial(load, g), lane, caches[g], masks)
                for u in range(t, min(t + 2, TILES))
            ]
            wide = jnp.concatenate(values, axis=1) if len(values) > 1 else values[0]
            ref[rows, 128 * t : 128 * t + wide.shape[1]] = wide


def match_kernel(
    images,
    refs,
    groups_far,
    table_far,
    precision_far,
    counts_far,
    stack,
    prob,
    stats,
    power_out,
    pix,
    raw,
    turned,
    scales,
    logits,
    groups,
    table,
    precision,
    counts,
    sems,
    small_sems,
):
    me = lax.axis_index("dom")
    small = [
        pltpu.make_async_copy(src, dst, small_sems.at[n])
        for n, (src, dst) in enumerate(
            (
                (groups_far, groups),
                (table_far, table),
                (precision_far, precision),
                (counts_far, counts),
            )
        )
    ]
    copies = []
    for i in range(CHUNKS):
        span = pl.ds(i * WIDE, WIDE)
        copies.append(pltpu.make_async_copy(refs.at[:, span], raw.at[i], sems.at[0, i]))
        copies.append(pltpu.make_async_copy(images.at[:, span], pix.at[i], sems.at[1, i]))
    small[3].start()
    copies[0].start()
    for copy in small[:3] + copies[1:]:
        copy.start()
    small[3].wait()

    lane_r = lax.broadcasted_iota(jnp.int32, (K_OWN, 128), 1)
    lane_e = lax.broadcasted_iota(jnp.int32, (K_OWN, CYCLES), 1)
    lane_w = lax.broadcasted_iota(jnp.int32, (16, 128), 1)
    nought = [jnp.minimum(counts[i], 0) for i in range(CHUNKS)]

    def turn_refs(i, energy):
        copies[2 * i].wait()
        tiles = [raw[i, :, 128 * t : 128 * t + 128] for t in range(TILES)]
        lane16 = (lane_r + nought[i]).astype(jnp.int16)
        for r2 in range(N2):
            plans = rolled_plan((SPAN - N1 * HOP * r2) % SPAN)
            rows = [slice(r2 * KP, r2 * KP + K_OWN)]
            store_tiles(turned.at[i % 2], rows, plans, lambda g, u: tiles[u], lane16)
        sums = [None] * CYC
        for t in range(TILES):
            square = jnp.square(tiles[t].astype(jnp.float32))
            lo, hi = 128 * t // SPAN, (128 * t + 127) // SPAN
            parts = [(lo, square)]
            if hi != lo:
                edge = hi * SPAN - 128 * t
                parts = [
                    (lo, jnp.where(lane_r < edge, square, 0.0)),
                    (hi, jnp.where(lane_r >= edge, square, 0.0)),
                ]
            for c, part in parts:
                sums[c] = part if sums[c] is None else sums[c] + part
        for c in range(CYC):
            total = jnp.sum(sums[c], axis=1, keepdims=True)
            energy = jnp.where(lane_e == i * CYC + c, total, energy)
        return energy

    def weigh_images(i):
        copies[2 * i + 1].wait()
        for j in range(READ // 16):
            rows = slice(16 * j, 16 * j + 16)
            factor = scales[i, rows, :]
            cols = [jnp.broadcast_to(factor[:, c : c + 1], (16, 128)) for c in range(CYC)]
            weighted = []
            for t in range(TILES):
                lo, hi = 128 * t // SPAN, (128 * t + 127) // SPAN
                amount = cols[lo]
                if hi != lo:
                    amount = jnp.where(lane_w < hi * SPAN - 128 * t, cols[lo], cols[hi])
                pixels = pix[i, rows, 128 * t : 128 * t + 128].astype(jnp.float32)
                weighted.append((amount * pixels).astype(jnp.bfloat16))
            stack[i, rows, :] = jnp.concatenate(weighted, axis=1)

    def turn_images(i, r1):
        lane16 = (lane_w + nought[i]).astype(jnp.int16)
        groups_in = [slice(16 * j, 16 * j + 16) for j in range(READ // 16)]
        groups_out = [
            slice(r1 * QP + 16 * j, r1 * QP + 16 * j + 16) for j in range(READ // 16)
        ]
        store_tiles(
            stack.at[i],
            groups_out,
            rolled_plan(HOP * r1),
            lambda g, u: stack[i, groups_in[g], 128 * u : 128 * u + 128],
            lane16,
        )

    def multiply(i, part):
        cols = slice(2 * QP * part, 2 * QP * (part + 1))
        value = None
        for span in (slice(0, 14 * 128), slice(14 * 128, WIDE)):
            piece = lax.dot_general(
                turned[i % 2, :, span],
                stack[i, cols, span],
                (((1,), (1,)), ((), ())),
                preferred_element_type=jnp.float32,
            )
            value = piece if value is None else value + piece
        if i:
            value = value + logits[:, cols]
        logits[:, cols] = value

    energy = turn_refs(0, jnp.zeros((K_OWN, CYCLES), jnp.float32))
    for copy in small[:3]:
        copy.wait()
    lane = lax.broadcasted_iota(jnp.int32, (8, QP), 1)
    base = me * READ
    row = base // 128
    off = base - row * 128
    turn = lax.rem(128 - off, 128)
    head = jnp.broadcast_to(groups[pl.ds(row, 1), :], (8, QP))
    tail = jnp.broadcast_to(groups[pl.ds(jnp.minimum(row + 1, 23), 1), :], (8, QP))
    mine = jnp.where(
        lane + off < 128, pltpu.roll(head, turn, axis=1), pltpu.roll(tail, turn, axis=1)
    )
    hot = (lax.broadcasted_iota(jnp.int32, (QP, QP), 0) == mine[0:1, :]).astype(jnp.float32)
    hot = hot.T[:, :GROUPS]
    ctf = jnp.dot(hot, table[...], precision=HIGH, preferred_element_type=jnp.float32)
    scale = precision[...] * ctf
    power = precision[...] * jnp.square(ctf)
    power_out[...] = power
    for i in range(CHUNKS):
        scales[i, :, 0:CYC] = scale[:, i * CYC : (i + 1) * CYC]

    for i in range(CHUNKS):
        if i:
            energy = turn_refs(i, energy)
            multiply(i - 1, 0)
        weigh_images(i)
        for r1 in range(1, N1):
            if i and r1 in (2, 4):
                multiply(i - 1, r1 // 2)
            turn_images(i, r1)
    for part in range(3):
        multiply(CHUNKS - 1, part)

    ref_power = lax.dot_general(
        energy,
        power,
        (((1,), (1,)), ((), ())),
        precision=HIGH,
        preferred_element_type=jnp.float32,
    )
    half = 0.5 * ref_power
    lane_q = lax.broadcasted_iota(jnp.int32, (K_OWN, QP), 1)
    alive = lane_q < counts[me]
    peak = jnp.full((K_OWN, QP), -3.0e38, jnp.float32)
    for r2 in range(N2):
        for r1 in range(N1):
            rows = slice(r2 * KP, r2 * KP + K_OWN)
            cols = slice(r1 * QP, (r1 + 1) * QP)
            value = jnp.where(alive, logits[rows, cols] - half, 0.0)
            logits[rows, cols] = value
            peak = jnp.maximum(peak, value)
    peak = jnp.max(peak, axis=0, keepdims=True)
    mass = jnp.zeros((K_OWN, QP), jnp.float32)
    prob[...] = jnp.zeros_like(prob)
    for r2 in range(N2):
        for r1 in range(N1):
            rows = slice(r2 * KP, r2 * KP + K_OWN)
            cols = slice(r1 * QP, (r1 + 1) * QP)
            value = jnp.exp(logits[rows, cols] - peak)
            prob[rows, cols] = value
            mass = mass + value
    mass = jnp.sum(mass, axis=0, keepdims=True)
    sub = lax.broadcasted_iota(jnp.int32, (8, QP), 0)
    block = jnp.where(sub == 0, peak, jnp.where(alive[0:1, :], mass, 0.0))
    stats[...] = block


def scatter_chunk(stack, post, dens, partial, out, x_to):
    rows = [stack[x_to, r1 * QP : r1 * QP + READ, :] for r1 in range(N1)]
    partial[...] = jnp.dot(
        post[...], jnp.concatenate(rows, axis=0), preferred_element_type=jnp.float32
    )
    lane = lax.broadcasted_iota(jnp.int32, (KP, 128), 1)
    caches = [{} for _ in range(N2)]
    for c in range(CYC):
        for part in range(4):
            total = None
            masks = {}
            for r2 in range(N2):
                value = gather_tile(
                    packed_plan(c, part, N1 * HOP * r2),
                    lambda u: partial[r2 * KP : (r2 + 1) * KP, 128 * u : 128 * u + 128],
                    lane,
                    caches[r2],
                    masks,
                )
                total = value if total is None else total + value
            if part == 3:
                total = jnp.where(lane == EDGE, dens[x_to][:, c : c + 1], total)
                high = pltpu.roll(total[LOW : 2 * LOW], 64, axis=1)
                total = jnp.where(lane[:LOW] < 64, total[:LOW], high)
                out[c, 3 * K_OWN : PACK, :] = total.astype(out.dtype)
            else:
                out[c, K_OWN * part : K_OWN * (part + 1), :] = total[:K_OWN].astype(out.dtype)


def first_chunk_kernel(
    hop, stack, prob, stats, pair, near, far, back, power, out, post, dens, conf, partial
):
    me = lax.axis_index("dom")
    pairs = (pair, near, far, back)
    peak = functools.reduce(jnp.maximum, [part[0:1, :] for part in pairs])
    masses = [part[1:2, :] * jnp.exp(part[0:1, :] - peak) for part in pairs]
    mass = (masses[0] + masses[1]) + (masses[2] + masses[3])
    alive = mass > 0.0
    own_peak = stats[0:1, :]
    factor = jnp.where(alive, jnp.exp(own_peak - peak) / mass, 0.0)
    conf[...] = jnp.where(alive, 1.0 / mass, 0.0)[:, :READ]
    total = jnp.zeros((KP, QP), jnp.float32)
    for r2 in range(N2):
        for r1 in range(N1):
            rows = slice(r2 * KP, (r2 + 1) * KP)
            cols = slice(r1 * QP, (r1 + 1) * QP)
            value = prob[rows, cols] * factor
            total = total + value
            post[rows, r1 * READ : (r1 + 1) * READ] = value[:, :READ].astype(jnp.bfloat16)
    den = jnp.dot(total, power[...], precision=HIGH, preferred_element_type=jnp.float32)
    for i in range(CHUNKS):
        dens[i, :, 0:CYC] = den[:, i * CYC : (i + 1) * CYC]
    scatter_chunk(stack, post, dens, partial, out, lax.rem(me // Z_SIZE + hop, X_SIZE))


def chunk_kernel(hop, stack, post, dens, out, partial):
    me = lax.axis_index("dom")
    scatter_chunk(stack, post, dens, partial, out, lax.rem(me // Z_SIZE + hop, X_SIZE))


def finish_kernel(pieces, out, acc):
    total = pieces[0].astype(jnp.float32)
    for i in range(1, Z_SIZE):
        total = total + pieces[i].astype(jnp.float32)
    acc[...] = total
    low = acc[3 * K_OWN : PACK, :]
    high = acc[3 * K_OWN : 4 * K_OWN - LOW, 64:128]
    den_low = low[:, EDGE : EDGE + 1] + ridge_term
    den_high = high[:, EDGE : EDGE + 1] + ridge_term
    den = jnp.concatenate([den_low, den_high], axis=0)
    for part in range(3):
        out[:, 128 * part : 128 * (part + 1)] = acc[K_OWN * part : K_OWN * (part + 1), :] / den
    out[0:LOW, 384:SPAN] = low[:, 0:EDGE] / den_low
    out[LOW:K_OWN, 384:SPAN] = high[:, 0:EDGE] / den_high


def in_hbm(x):
    return pltpu.with_memory_space_constraint(x, pltpu.HBM)


def in_vmem(x):
    return pltpu.with_memory_space_constraint(x, pltpu.VMEM)


def body(images, pick_counts, group_of, ctf_table, precision, references):
    f32, bf16 = jnp.float32, jnp.bfloat16
    operands = (
        images,
        references,
        group_of.reshape(24, 128),
        ctf_table,
        precision.reshape(1, CYCLES),
        pick_counts,
    )
    stack, prob, stats, power = pl.pallas_call(
        match_kernel,
        out_shape=(
            pltpu.VMEM((CHUNKS, N1 * QP, WIDE), bf16),
            pltpu.VMEM((N2 * KP, N1 * QP), f32),
            jax.ShapeDtypeStruct((8, QP), f32),
            pltpu.VMEM((QP, CYCLES), f32),
        ),
        in_specs=[FAR] * 6,
        out_specs=(VM, VM, VM, VM),
        scratch_shapes=[
            pltpu.VMEM((CHUNKS, READ, WIDE), bf16),
            pltpu.VMEM((CHUNKS, K_OWN, WIDE), bf16),
            pltpu.VMEM((2, N2 * KP, WIDE), bf16),
            pltpu.VMEM((CHUNKS, QP, 128), f32),
            pltpu.VMEM((N2 * KP, N1 * QP), f32),
            pltpu.VMEM((24, 128), jnp.int32),
            pltpu.VMEM((GROUPS, CYCLES), f32),
            pltpu.VMEM((1, CYCLES), f32),
            pltpu.SMEM((32,), jnp.int32),
            pltpu.SemaphoreType.DMA((2, CHUNKS)),
            pltpu.SemaphoreType.DMA((4,)),
        ],
        compiler_params=PARAMS,
        name="match",
    )(*map(in_hbm, operands))

    def swapped(x, bits):
        return lax.ppermute(x, "cls", [(j, j ^ bits) for j in range(8)])

    other = swapped(stats, 1)
    top = jnp.maximum(stats[0:1], other[0:1])
    both = stats * jnp.exp(stats[0:1] - top) + other * jnp.exp(other[0:1] - top)
    pair = jnp.where(jnp.arange(8)[:, None] == 0, top, both)
    seats = [pair] + [swapped(pair, bits) for bits in (2, 4, 6)]
    stack, prob, power = in_vmem(stack), in_vmem(prob), in_vmem(power)

    part_shape = (CYC, PACK, 128)
    partial = pltpu.VMEM((N2 * KP, WIDE), f32)
    across, post, dens, conf = pl.pallas_call(
        functools.partial(first_chunk_kernel, 2),
        out_shape=(
            jax.ShapeDtypeStruct(part_shape, bf16),
            pltpu.VMEM((N2 * KP, N1 * READ), bf16),
            pltpu.VMEM((CHUNKS, KP, 128), f32),
            jax.ShapeDtypeStruct((1, READ), f32),
        ),
        in_specs=[VM] * 8,
        out_specs=(VM, VM, VM, VM),
        scratch_shapes=[partial],
        compiler_params=PARAMS,
        name="chunk2",
    )(stack, prob, stats, *seats, power)
    post, dens = in_vmem(post), in_vmem(dens)

    def moved(piece, hop):
        ring = [(j, (j // Z_SIZE + hop) % X_SIZE * Z_SIZE + j % Z_SIZE) for j in range(32)]
        return lax.ppermute(piece, "dom", ring)

    def chunk_call(hop, dtype):
        return pl.pallas_call(
            functools.partial(chunk_kernel, hop),
            out_shape=jax.ShapeDtypeStruct(part_shape, dtype),
            in_specs=[VM, VM, VM],
            out_specs=VM,
            scratch_shapes=[partial],
            compiler_params=PARAMS,
        )(stack, post, dens)

    got2 = moved(across, 2)
    got1 = moved(chunk_call(1, bf16), 1)
    got3 = moved(chunk_call(3, bf16), 3)
    own = chunk_call(0, f32)
    total = own + got1.astype(f32) + got2.astype(f32) + got3.astype(f32)
    z_groups = [[x * Z_SIZE + z for z in range(Z_SIZE)] for x in range(X_SIZE)]
    pieces = lax.all_to_all(total.astype(bf16), "dom", 0, 0, axis_index_groups=z_groups)
    new_refs = pl.pallas_call(
        finish_kernel,
        out_shape=jax.ShapeDtypeStruct((K_OWN, SPAN), f32),
        in_specs=[VM],
        out_specs=VM,
        scratch_shapes=[pltpu.VMEM((PACK, 128), f32)],
        compiler_params=PARAMS,
        name="finish",
    )(pieces)
    return new_refs, conf.reshape(READ)


def solution(mesh):
    return jax.shard_map(
        body,
        mesh=mesh,
        in_specs=(P("dom", None), P(), P(), P(), P(), P("cls", None)),
        out_specs=(P("cls", "dom"), P("dom")),
        check_vma=False,
    )
```
